512 devices in a mesh: row: 16 (over z, core), col: 32 (over x, y).
Axes of the slice: x: 4, y: 8, z: 8, core: 2. Of those that a mesh axis runs over, the one named last changes fastest.
Arguments:
- state_fields: bfloat16 [4, 16, 16, 16, 32, 256], P(None, None, None, 'row', 'col'), may hold values from -6 to 6
- leaf_solve: float32 [256, 256], replicated, may hold values from -0.375 to 0.375
- leaf_flux: float32 [64, 256], replicated, may hold values from -0.375 to 0.375
- lift_edges: float32 [64, 128], replicated, may hold values from -4 to 4
- lift_leaves: float32 [256, 128], replicated, may hold values from -0.046875 to 0.046875
- merge_interface: float32 [5, 128, 128], replicated, may hold values from -0.25 to 0.25
- merge_parent: float32 [5, 256, 128], replicated, may hold values from -0.375 to 0.375
- split_child: float32 [5, 128, 256], replicated, may hold values from -0.5 to 0.5
- top_inverse: float32 [2048, 2048], P(None, 'row'), may hold values from -0.125 to 0.125
- spread_edges: float32 [64, 128], replicated, may hold values from -4 to 4
- spread_leaves: float32 [256, 128], replicated, may hold values from -0.5 to 0.5
- leaf_extend: float32 [256, 64], replicated, may hold values from -0.375 to 0.375
Outputs:
- new_fields: bfloat16 [4, 16, 16, 16, 32, 256], P(None, None, None, 'row', 'col')
The draws below stay inside these ranges and needn't reach their ends.
All inputs are finite; a program needn't handle non-finite values.
Results may differ from the reference program's by a relative error of at most 0.0035.
Values may be sent and summed in bfloat16 or wider, within the bound.
A program may use at most 64 MiB of HBM per device.

```python
import jax
import jax.numpy as jnp
import numpy as np
from jax import lax

NODE = 16
FIELDS = 4
SKEL = 128
LR = 4
LC = 64
NN = 256
EDGE = 64
LEAVES = 256
LEVELS = 5
N_ROW = 16
N_COL = 32


def levels(own_key, extent, split, least, largest):
    factor_of, own = 1.0, jax.random.fold_in(own_key, 6)
    for axis_at, shards_of in split:
        draws = jnp.exp(jax.random.uniform(jax.random.fold_in(own, axis_at), (shards_of,), jnp.float32, least / len(split), largest / len(split)))
        factor_of = factor_of * jnp.repeat(draws, extent[axis_at] // shards_of).reshape([-1 if axis == axis_at else 1 for axis in range(len(extent))])
    return factor_of


def centred(key, extent, scale, bound, shards=(), held_as=jnp.bfloat16):
    array = jax.random.normal(key, extent, jnp.float32) * scale
    if len(shards) > 0:
        array = levels(key, extent, shards, -0.22, 0.18) * array
    return jnp.clip(array, min=-bound, max=bound).astype(held_as)


def setup_inputs(seed: int = 0) -> dict:
    streams_of = jax.random.split(jax.random.key(seed), 13)
    state_fields = centred(streams_of[0], (FIELDS, NODE, NODE, N_ROW, N_COL, LEAVES), 1.0, 6.0, ((3, 16), (4, 32)))
    leaf_solve = centred(streams_of[1], (NN, NN), NN ** -0.5, 0.375, (), jnp.float32)
    leaf_flux = centred(streams_of[2], (EDGE, NN), NN ** -0.5, 0.375, (), jnp.float32)
    lift_edges = centred(streams_of[3], (EDGE, SKEL), 1.0, 4.0, (), jnp.float32)
    lift_leaves = centred(streams_of[4], (LEAVES, SKEL), (EDGE * LEAVES) ** -0.5, 0.046875, (), jnp.float32)
    merge_interface = centred(streams_of[5], (LEVELS, SKEL, SKEL), (4 * SKEL) ** -0.5, 0.25, (), jnp.float32)
    merge_parent = centred(streams_of[6], (LEVELS, 2 * SKEL, SKEL), (2 * SKEL) ** -0.5, 0.375, (), jnp.float32)
    split_child = centred(streams_of[7], (LEVELS, SKEL, 2 * SKEL), SKEL ** -0.5, 0.5, (), jnp.float32)
    top_inverse = centred(streams_of[8], (N_ROW * SKEL, N_ROW * SKEL), (N_ROW * SKEL) ** -0.5, 0.125, ((1, 16),), jnp.float32)
    spread_edges = centred(streams_of[9], (EDGE, SKEL), 1.0, 4.0, (), jnp.float32)
    spread_leaves = centred(streams_of[10], (LEAVES, SKEL), SKEL ** -0.5, 0.5, (), jnp.float32)
    leaf_extend = centred(streams_of[11], (NN, EDGE), (4 * EDGE) ** -0.5, 0.375, (), jnp.float32)
    return {"state_fields": state_fields, "leaf_solve": leaf_solve, "leaf_flux": leaf_flux, "lift_edges": lift_edges, "lift_leaves": lift_leaves, "merge_interface": merge_interface, "merge_parent": merge_parent, "split_child": split_child, "top_inverse": top_inverse, "spread_edges": spread_edges, "spread_leaves": spread_leaves, "leaf_extend": leaf_extend}


advect_scale = 0.01
full_precision = lax.Precision.HIGHEST


def chebyshev_matrix(node_count):
    points = np.arange(node_count)
    grid_x = np.cos(np.pi * points / (node_count - 1))
    weights = np.where(points == 0, 2.0, np.where(points == node_count - 1, 2.0, 1.0))
    parity = np.where((points[:, None] + points[None, :]) % 2 == 0, 1.0, -1.0)
    identity = np.eye(node_count)
    spacing = grid_x[:, None] - grid_x[None, :] + identity
    off_diagonal = (weights[:, None] / weights[None, :]) * parity / spacing * (1.0 - identity)
    result_matrix = off_diagonal - identity * off_diagonal.sum(axis=1)[:, None]
    return jnp.asarray(result_matrix, dtype=jnp.float32)


def average_rows(values, north_in, south_in):
    above = jnp.concatenate([north_in, values[:, -1, :, :-1, :]], axis=2)
    below = jnp.concatenate([values[:, 0, :, 1:, :], south_in], axis=2)
    first_row = (values[:, 0] + above) * 0.5
    last_row = (values[:, -1] + below) * 0.5
    return jnp.concatenate([first_row[:, None], values[:, 1:-1], last_row[:, None]], axis=1)


def average_cols(values, west_in, east_in):
    left_side = jnp.concatenate([west_in, values[:, :, -1, :, :-1]], axis=3)
    right_side = jnp.concatenate([values[:, :, 0, :, 1:], east_in], axis=3)
    first_col = (values[:, :, 0] + left_side) * 0.5
    last_col = (values[:, :, -1] + right_side) * 0.5
    return jnp.concatenate([first_col[:, :, None], values[:, :, 1:-1], last_col[:, :, None]], axis=2)


def reference(state_fields, leaf_solve, leaf_flux, lift_edges, lift_leaves, merge_interface, merge_parent, split_child, top_inverse, spread_edges, spread_leaves, leaf_extend):
    field_count = state_fields.shape[0]
    node_count = state_fields.shape[1]
    node_total = node_count * node_count
    leaf_total = LR * LC
    grid_values = state_fields.astype(jnp.float32).reshape(field_count, node_count, node_count, N_ROW, N_COL, LR, LC)
    grid_values = jnp.transpose(grid_values, (0, 1, 2, 3, 5, 4, 6)).reshape(field_count, node_count, node_count, N_ROW * LR, N_COL * LC)
    derivative = chebyshev_matrix(node_count)
    velocity_x = grid_values[0]
    velocity_y = grid_values[1]

    def one_field(field_values):
        along_rows = jnp.einsum('ik,kjrc->ijrc', derivative, field_values, precision=full_precision)
        along_cols = jnp.einsum('jk,ikrc->ijrc', derivative, field_values, precision=full_precision)
        return advect_scale * (velocity_x * along_rows + velocity_y * along_cols)

    pushed = lax.map(one_field, grid_values)
    rows_done = average_rows(pushed, pushed[:, -1][:, :, -1:, :], pushed[:, 0][:, :, :1, :])
    averaged = average_cols(rows_done, rows_done[:, :, -1][:, :, :, -1:], rows_done[:, :, 0][:, :, :, :1])
    source = (grid_values - averaged).reshape(field_count, node_count, node_count, N_ROW, LR, N_COL, LC)
    source = jnp.transpose(source, (3, 5, 0, 1, 2, 4, 6)).reshape(N_ROW, N_COL, field_count, node_total, leaf_total)

    def row_section(row_source):
        particular = jnp.einsum('nm,cfml->cfnl', leaf_solve, row_source, precision=full_precision)
        edge_flux = jnp.einsum('em,cfml->cfel', leaf_flux, row_source, precision=full_precision)
        lifted = jnp.einsum('cfel,lb->cfeb', edge_flux, lift_leaves, precision=full_precision)
        skeleton = jnp.sum(lifted * lift_edges[None, None], axis=2)
        return particular, skeleton

    particular, skeleton = lax.map(row_section, source)
    interfaces = []
    for merge_level in range(LEVELS):
        paired = skeleton.reshape(N_ROW, -1, 2, field_count, SKEL)
        left_half = paired[:, :, 0]
        right_half = paired[:, :, 1]
        interfaces.append(jnp.einsum('rpfb,bc->rpfc', right_half - left_half, merge_interface[merge_level], precision=full_precision))
        joined = jnp.concatenate([left_half, right_half], axis=-1)
        skeleton = jnp.einsum('rpfb,bc->rpfc', joined, merge_parent[merge_level], precision=full_precision)
    top_matrix = top_inverse.reshape(N_ROW, SKEL, N_ROW, SKEL)
    boundary = jnp.einsum('gfb,gbrc->rfc', skeleton[:, 0], top_matrix, precision=full_precision)[:, None]
    for merge_level in reversed(range(LEVELS)):
        child_map = split_child[merge_level]
        left_half = jnp.einsum('rpfb,bc->rpfc', boundary, child_map[:, :SKEL], precision=full_precision) + interfaces[merge_level]
        right_half = jnp.einsum('rpfb,bc->rpfc', boundary, child_map[:, SKEL:], precision=full_precision) + interfaces[merge_level]
        boundary = jnp.stack([left_half, right_half], axis=2).reshape(N_ROW, -1, field_count, SKEL)

    def row_finish(row_pair):
        row_particular, row_boundary = row_pair
        weighted = row_boundary[:, :, None, :] * spread_edges[None, None]
        spread = jnp.einsum('cfeb,lb->cfel', weighted, spread_leaves, precision=full_precision)
        return row_particular + jnp.einsum('ne,cfel->cfnl', leaf_extend, spread, precision=full_precision)

    solved = lax.map(row_finish, (particular, boundary))
    solved = jnp.transpose(solved, (2, 3, 0, 1, 4)).reshape(field_count, node_count, node_count, N_ROW, N_COL, leaf_total)
    return solved.astype(jnp.bfloat16)
```

```python
import jax
import jax.numpy as jnp
import numpy as np
from jax import lax
from jax.experimental import pallas as pl
from jax.experimental.pallas import tpu as pltpu
from jax.sharding import PartitionSpec as P

F32 = jnp.float32
BF16 = jnp.bfloat16
MESH = pl.DeviceIdType.MESH
LEVELS = 5
N_ROW = 16
N_COL = 32
advect_scale = 0.01


def chebyshev_matrix(node_count):
    points = np.arange(node_count)
    grid_x = np.cos(np.pi * points / (node_count - 1))
    weights = np.where(points == 0, 2.0, np.where(points == node_count - 1, 2.0, 1.0))
    parity = np.where((points[:, None] + points[None, :]) % 2 == 0, 1.0, -1.0)
    identity = np.eye(node_count)
    spacing = grid_x[:, None] - grid_x[None, :] + identity
    off_diagonal = weights[:, None] / weights[None, :] * parity / spacing * (1.0 - identity)
    result_matrix = off_diagonal - identity * off_diagonal.sum(axis=1)[:, None]
    return result_matrix.astype(np.float32)


def derivative_parts():
    d = chebyshev_matrix(16)
    eye = np.eye(16, dtype=np.float32)
    both = np.concatenate([np.kron(d, eye), np.kron(eye, d)], axis=0) * np.float32(advect_scale)
    high = both.astype(jnp.bfloat16)
    low = (both - high.astype(np.float32)).astype(jnp.bfloat16)
    return high, low


def face_columns():
    e = np.zeros((256, 64), np.float32)
    for k in range(16):
        e[k, k] = 1.0
        e[240 + k, 16 + k] = 1.0
        e[16 * k, 32 + k] = 1.0
        e[16 * k + 15, 48 + k] = 1.0
    return e.astype(jnp.bfloat16)


def split(x):
    high = x.astype(BF16)
    return high, (x - high.astype(F32)).astype(BF16)


def mm(a, b, dims=((1,), (0,))):
    return lax.dot_general(a, b, (dims, ((), ())), preferred_element_type=F32)


def dot3(a, b, dims=((1,), (0,))):
    return mm(a[0], b[0], dims) + mm(a[0], b[1], dims) + mm(a[1], b[0], dims)


def bit_reversed(m):
    return sum(((m >> k) & 1) << (LEVELS - 1 - k) for k in range(LEVELS))


def kernel(
    q_ref, solve_ref, flux_ref, lift_e_ref, lift_l_ref, mi_ref, parent_ref, child_ref, top_ref,
    spr_e_ref, spr_l_ref, ext_t_ref, der_h_ref, der_l_ref, face_ref,
    out_ref,
    tend_ref, part_ref, k_ref, src1, dst1, src2, dst2, src3, dst3, src4, dst4,
    par_h, par_l, top_h, top_l,
    send1, recv1, send2, recv2, send3, recv3, send4, recv4,
):
    row = lax.axis_index("row")
    col = lax.axis_index("col")
    bits = [(col // (1 << k)) % 2 for k in range(LEVELS)]

    def other(m):
        return sum(
            (1 - bits[k] if (m >> k) & 1 else bits[k]) * (1 << k) for k in range(LEVELS)
        )

    def row_at(d):
        return (row + d) % N_ROW

    barrier = pltpu.get_barrier_semaphore()
    for m in range(1, N_COL):
        pl.semaphore_signal(barrier, inc=1, device_id=(row, other(m)), device_id_type=MESH)
    for d in range(1, N_ROW):
        pl.semaphore_signal(barrier, inc=1, device_id=(row_at(d), col), device_id_type=MESH)

    der_h, der_l = der_h_ref[...], der_l_ref[...]
    q0 = q_ref[0:256, :].astype(F32)
    q1 = q_ref[256:512, :].astype(F32)
    for f in range(4):
        q = q_ref[256 * f : 256 * f + 256, :]
        both = mm(der_h, q) + mm(der_l, q)
        tend_ref[256 * f : 256 * f + 256, :] = q0 * both[:256] + q1 * both[256:]

    lane = lax.broadcasted_iota(jnp.int32, (64, 256), 1)
    half_lane = lax.broadcasted_iota(jnp.int32, (64, 128), 1)
    place = lax.broadcasted_iota(jnp.int32, (64, 256), 0) % 16

    def rows_of(first):
        return jnp.concatenate(
            [tend_ref[256 * f + first : 256 * f + first + 16, :] for f in range(4)], axis=0
        )

    def nodes_of(first):
        return tend_ref[...].reshape(64, 16, 256)[:, first, :]

    top, bottom = rows_of(0), rows_of(240)
    above = pltpu.roll(bottom, 64, 1)
    below = pltpu.roll(top, 192, 1)
    src1[0] = above[:, :128]
    src1[1] = below[:, 128:]
    pl.semaphore_wait(barrier, N_COL - 1 + N_ROW - 1)

    def remote(src, dst, send, recv, where):
        return pltpu.make_async_remote_copy(
            src_ref=src, dst_ref=dst, send_sem=send, recv_sem=recv, device_id=where,
            device_id_type=MESH,
        )

    south = remote(src1.at[0], dst1.at[0], send1.at[0], recv1.at[0], (row_at(1), col))
    north = remote(src1.at[1], dst1.at[1], send1.at[1], recv1.at[1], (row_at(N_ROW - 1), col))
    south.start()
    north.start()

    k_map = dot3(
        split(flux_ref[...].T), split(lift_e_ref[...])
    )
    k_ref[...] = k_map
    lift_l = split(lift_l_ref[...])
    own = []
    for f in range(4):
        q = q_ref[256 * f : 256 * f + 256, :].astype(F32)
        w = dot3(split(q - tend_ref[256 * f : 256 * f + 256, :]), lift_l)
        own.append(jnp.sum(w * k_map, axis=0, keepdims=True))
    left, right = nodes_of(0), nodes_of(15)

    south.wait()
    north.wait()
    above = jnp.where(lane < 64, jnp.concatenate([dst1[0], dst1[0]], axis=1), above)
    below = jnp.where(lane >= 192, jnp.concatenate([dst1[1], dst1[1]], axis=1), below)
    top_new = (top + above) * 0.5
    bottom_new = (bottom + below) * 0.5
    left_rows = jnp.where(
        place == 0, top_new, jnp.where(place == 15, pltpu.roll(bottom_new, 15, 0), left)
    )
    right_rows = jnp.where(
        place == 0, pltpu.roll(top_new, 49, 0), jnp.where(place == 15, bottom_new, right)
    )
    to_east = pltpu.roll(right_rows, 193, 1)
    to_west = pltpu.roll(left_rows, 63, 1)
    src2[0] = jnp.where(half_lane % 64 == 0, to_east[:, :128], pltpu.roll(to_east[:, 128:], 1, 1))
    src2[1] = jnp.where(half_lane % 64 == 63, to_west[:, :128], pltpu.roll(to_west[:, 128:], 1, 1))
    east = remote(src2.at[0], dst2.at[0], send2.at[0], recv2.at[0], (row, (col + 1) % N_COL))
    west = remote(
        src2.at[1], dst2.at[1], send2.at[1], recv2.at[1], (row, (col + N_COL - 1) % N_COL)
    )
    east.start()
    west.start()

    for k in range(LEVELS):
        whole = parent_ref[k]
        swapped = jnp.concatenate([whole[128:], whole[:128]], axis=0)
        high, low = split(jnp.where(bits[k] == 0, whole, swapped))
        par_h[k] = high
        par_l[k] = low

    east.wait()
    west.wait()

    def opened(received):
        return jnp.concatenate([received, pltpu.roll(received, 127, 1)], axis=1)

    before = jnp.where(lane % 64 == 0, opened(dst2[0]), pltpu.roll(right_rows, 1, 1))
    after = jnp.where(lane % 64 == 63, opened(dst2[1]), pltpu.roll(left_rows, 255, 1))
    inner = jnp.logical_and(place != 0, place != 15)
    deltas = [
        jnp.where(inner, top_new - top, 0.0),
        jnp.where(inner, bottom_new - bottom, 0.0),
        (left_rows + before) * 0.5 - left,
        (right_rows + after) * 0.5 - right,
    ]
    w = dot3(split(jnp.concatenate(deltas, axis=0)), lift_l)
    k_nodes = k_ref[...].reshape(16, 16, 128)
    k_faces = [k_nodes[0], k_nodes[15], k_nodes[:, 0, :], k_nodes[:, 15, :]]
    skeleton = []
    for f in range(4):
        change = sum(
            w[64 * s + 16 * f : 64 * s + 16 * f + 16] * k_faces[s] for s in range(4)
        )
        skeleton.append(own[f] - jnp.sum(change, axis=0, keepdims=True))
    skeleton = jnp.concatenate(skeleton, axis=0)
    src3[...] = skeleton
    dst3[0] = skeleton
    gathers = []
    for m in range(N_COL - 1, 0, -1):
        slot = bit_reversed(m)
        gathers.append(
            remote(src3, dst3.at[slot], send3.at[m], recv3.at[m], (row, other(m)))
        )
    for copy in gathers:
        copy.start()

    solve = split(solve_ref[...])
    face = face_ref[...]
    solve_face = (mm(solve[0], face).astype(BF16), mm(solve[1], face).astype(BF16))
    for f in range(4):
        q = q_ref[256 * f : 256 * f + 256, :].astype(F32)
        change = jnp.concatenate([d[16 * f : 16 * f + 16] for d in deltas], axis=0)
        part_ref[256 * f : 256 * f + 256, :] = dot3(
            solve, split(q - tend_ref[256 * f : 256 * f + 256, :])
        ) - dot3(solve_face, split(change))
    chain = None
    interface_maps = []
    for k in range(LEVELS):
        child = split(jnp.where(bits[k] == 0, child_ref[k, :, :128], child_ref[k, :, 128:]))
        sign = (1 - 2 * bits[k]).astype(F32)
        step = mi_ref[k] if chain is None else dot3(split(mi_ref[k]), chain)
        interface_maps.append(step * sign)
        chain = child if chain is None else split(dot3(child, chain))
    interface_map = split(jnp.concatenate(interface_maps, axis=0))
    for part in range(8):
        at = slice(256 * part, 256 * part + 256)
        high, low = split(dot3(split(top_ref[at, :]), chain))
        top_h[at, :] = high
        top_l[at, :] = low
    extend = dot3(split(ext_t_ref[...].T), split(spr_e_ref[...]))
    spread_l = split(spr_l_ref[...])

    for copy in gathers:
        copy.wait()
    x = dst3[...].reshape(4 * N_COL, 128)
    differences = []
    for k in range(LEVELS):
        rows = (4 * N_COL) >> (k + 1)
        first, second = x[:rows], x[rows:]
        differences.append((second - first)[:4])
        joined = jnp.concatenate([first, second], axis=1)
        x = dot3(split(joined), (par_h[k], par_l[k]))
    src4[...] = x
    dst4[row] = x
    sends = []
    arrivals = []
    for d in range(1, N_ROW):
        sends.append(remote(src4, dst4.at[row], send4.at[d], recv4.at[d], (row_at(d), col)))
        arrivals.append(
            remote(src4, dst4.at[row_at(N_ROW - d)], send4.at[d], recv4.at[d], (row_at(d), col))
        )
    for copy in sends:
        copy.start()
    boundary = dot3(split(jnp.concatenate(differences, axis=1)), interface_map)
    for copy in sends:
        copy.wait_send()
    for copy in arrivals:
        copy.wait_recv()
    pieces = split(jnp.concatenate([dst4[g] for g in range(N_ROW)], axis=1))
    boundary = boundary + dot3(pieces, (top_h[...], top_l[...]))
    for f in range(4):
        weighted = split(extend * boundary[f : f + 1, :])
        at = slice(256 * f, 256 * f + 256)
        out_ref[at, :] = (part_ref[at, :] + dot3(weighted, spread_l, ((1,), (1,)))).astype(BF16)


def local(
    state_fields, leaf_solve, leaf_flux, lift_edges, lift_leaves, merge_interface, merge_parent,
    split_child, top_inverse, spread_edges, spread_leaves, leaf_extend,
):
    der_h, der_l = derivative_parts()
    dma = pltpu.SemaphoreType.DMA
    result = pl.pallas_call(
        kernel,
        name="imex_step",
        out_shape=jax.ShapeDtypeStruct((1024, 256), BF16),
        in_specs=[pl.BlockSpec(memory_space=pltpu.VMEM)] * 15,
        out_specs=pl.BlockSpec(memory_space=pltpu.VMEM),
        scratch_shapes=[
            pltpu.VMEM((1024, 256), F32),
            pltpu.VMEM((1024, 256), F32),
            pltpu.VMEM((256, 128), F32),
            pltpu.VMEM((2, 64, 128), F32),
            pltpu.VMEM((2, 64, 128), F32),
            pltpu.VMEM((2, 64, 128), F32),
            pltpu.VMEM((2, 64, 128), F32),
            pltpu.VMEM((4, 128), F32),
            pltpu.VMEM((N_COL, 4, 128), F32),
            pltpu.VMEM((4, 128), F32),
            pltpu.VMEM((N_ROW, 4, 128), F32),
            pltpu.VMEM((LEVELS, 256, 128), BF16),
            pltpu.VMEM((LEVELS, 256, 128), BF16),
            pltpu.VMEM((2048, 128), BF16),
            pltpu.VMEM((2048, 128), BF16),
            dma((2,)), dma((2,)), dma((2,)), dma((2,)),
            dma((N_COL,)), dma((N_COL,)), dma((N_ROW,)), dma((N_ROW,)),
        ],
        compiler_params=pltpu.CompilerParams(
            collective_id=0, has_side_effects=True, vmem_limit_bytes=48 * 1024 * 1024
        ),
    )(
        state_fields.reshape(1024, 256), leaf_solve, leaf_flux, lift_edges, lift_leaves,
        merge_interface, merge_parent, split_child, top_inverse, spread_edges, spread_leaves,
        leaf_extend.T, jnp.asarray(der_h), jnp.asarray(der_l), jnp.asarray(face_columns()),
    )
    return result.reshape(state_fields.shape)


def solution(mesh):
    in_specs = (
        P(None, None, None, "row", "col", None),
        P(), P(), P(), P(), P(), P(), P(),
        P(None, "row"),
        P(), P(), P(),
    )
    out_specs = P(None, None, None, "row", "col", None)
    return jax.shard_map(local, mesh=mesh, in_specs=in_specs, out_specs=out_specs, check_vma=False)
```

```python
import jax
import jax.numpy as jnp
import numpy as np
from jax import lax
from jax.experimental import pallas as pl
from jax.experimental.pallas import tpu as pltpu
from jax.sharding import PartitionSpec as P

F32 = jnp.float32
BF16 = jnp.bfloat16
MESH = pl.DeviceIdType.MESH
LEVELS = 5
N_ROW = 16
N_COL = 32
advect_scale = 0.01


def chebyshev_matrix(node_count):
    points = np.arange(node_count)
    grid_x = np.cos(np.pi * points / (node_count - 1))
    weights = np.where(points == 0, 2.0, np.where(points == node_count - 1, 2.0, 1.0))
    parity = np.where((points[:, None] + points[None, :]) % 2 == 0, 1.0, -1.0)
    identity = np.eye(node_count)
    spacing = grid_x[:, None] - grid_x[None, :] + identity
    off_diagonal = weights[:, None] / weights[None, :] * parity / spacing * (1.0 - identity)
    result_matrix = off_diagonal - identity * off_diagonal.sum(axis=1)[:, None]
    return result_matrix.astype(np.float32)


def derivative_parts():
    d = chebyshev_matrix(16)
    eye = np.eye(16, dtype=np.float32)
    both = np.concatenate([np.kron(d, eye), np.kron(eye, d)], axis=0) * np.float32(advect_scale)
    high = both.astype(jnp.bfloat16)
    low = (both - high.astype(np.float32)).astype(jnp.bfloat16)
    return high, low


def face_columns():
    e = np.zeros((256, 64), np.float32)
    for k in range(16):
        e[k, k] = 1.0
        e[240 + k, 16 + k] = 1.0
        e[16 * k, 32 + k] = 1.0
        e[16 * k + 15, 48 + k] = 1.0
    return e.astype(jnp.bfloat16)


def split(x):
    high = x.astype(BF16)
    return high, (x - high.astype(F32)).astype(BF16)


def mm(a, b, dims=((1,), (0,))):
    return lax.dot_general(a, b, (dims, ((), ())), preferred_element_type=F32)


def dot3(a, b, dims=((1,), (0,))):
    return mm(a[0], b[0], dims) + mm(a[0], b[1], dims) + mm(a[1], b[0], dims)


def bit_reversed(m):
    return sum(((m >> k) & 1) << (LEVELS - 1 - k) for k in range(LEVELS))


def kernel(*refs):
    stored, out_ref, held, loaded = refs[:15], refs[15], refs[16:31], refs[31]
    step(stored, held, loaded, out_ref, *refs[32:])


def step(
    stored, held, loaded, out_ref,
    tend_ref, part_ref, k_ref, src1, dst1, src2, dst2, src3, dst3, src4, dst4,
    par_h, par_l, top_h, top_l,
    send1, recv1, send2, recv2, send3, recv3, send4, recv4,
):
    row = lax.axis_index("row")
    col = lax.axis_index("col")
    bits = [(col // (1 << k)) % 2 for k in range(LEVELS)]

    def other(m):
        return sum(
            (1 - bits[k] if (m >> k) & 1 else bits[k]) * (1 << k) for k in range(LEVELS)
        )

    def row_at(d):
        return (row + d) % N_ROW

    barrier = pltpu.get_barrier_semaphore()
    for m in range(1, N_COL):
        pl.semaphore_signal(barrier, inc=1, device_id=(row, other(m)), device_id_type=MESH)
    for d in range(1, N_ROW):
        pl.semaphore_signal(barrier, inc=1, device_id=(row_at(d), col), device_id_type=MESH)

    (
        q_ref, solve_ref, flux_ref, lift_e_ref, lift_l_ref, mi_ref, parent_ref, child_ref,
        top_ref, spr_e_ref, spr_l_ref, ext_t_ref, der_h_ref, der_l_ref, face_ref,
    ) = held
    loads = [
        pltpu.make_async_copy(stored[i], held[i], loaded.at[i]) for i in range(15)
    ]
    for i in (0, 12, 13, 2, 3, 4, 6, 1, 14, 5, 7, 8, 11, 9, 10):
        loads[i].start()

    def arrived(*which):
        for i in which:
            loads[i].wait()

    arrived(0, 12, 13)
    der_h, der_l = der_h_ref[...], der_l_ref[...]
    q0 = q_ref[0:256, :].astype(F32)
    q1 = q_ref[256:512, :].astype(F32)
    for f in range(4):
        q = q_ref[256 * f : 256 * f + 256, :]
        both = mm(der_h, q) + mm(der_l, q)
        tend_ref[256 * f : 256 * f + 256, :] = q0 * both[:256] + q1 * both[256:]

    lane = lax.broadcasted_iota(jnp.int32, (64, 256), 1)
    half_lane = lax.broadcasted_iota(jnp.int32, (64, 128), 1)
    place = lax.broadcasted_iota(jnp.int32, (64, 256), 0) % 16

    def rows_of(first):
        return jnp.concatenate(
            [tend_ref[256 * f + first : 256 * f + first + 16, :] for f in range(4)], axis=0
        )

    def nodes_of(first):
        return tend_ref[...].reshape(64, 16, 256)[:, first, :]

    top, bottom = rows_of(0), rows_of(240)
    above = pltpu.roll(bottom, 64, 1)
    below = pltpu.roll(top, 192, 1)
    src1[0] = above[:, :128]
    src1[1] = below[:, 128:]
    pl.semaphore_wait(barrier, N_COL - 1 + N_ROW - 1)

    def remote(src, dst, send, recv, where):
        return pltpu.make_async_remote_copy(
            src_ref=src, dst_ref=dst, send_sem=send, recv_sem=recv, device_id=where,
            device_id_type=MESH,
        )

    south = remote(src1.at[0], dst1.at[0], send1.at[0], recv1.at[0], (row_at(1), col))
    north = remote(src1.at[1], dst1.at[1], send1.at[1], recv1.at[1], (row_at(N_ROW - 1), col))
    south.start()
    north.start()

    arrived(2, 3, 4)
    k_map = dot3(
        split(flux_ref[...].T), split(lift_e_ref[...])
    )
    k_ref[...] = k_map
    lift_l = split(lift_l_ref[...])
    own = []
    for f in range(4):
        q = q_ref[256 * f : 256 * f + 256, :].astype(F32)
        w = dot3(split(q - tend_ref[256 * f : 256 * f + 256, :]), lift_l)
        own.append(jnp.sum(w * k_map, axis=0, keepdims=True))
    left, right = nodes_of(0), nodes_of(15)

    south.wait()
    north.wait()
    above = jnp.where(lane < 64, jnp.concatenate([dst1[0], dst1[0]], axis=1), above)
    below = jnp.where(lane >= 192, jnp.concatenate([dst1[1], dst1[1]], axis=1), below)
    top_new = (top + above) * 0.5
    bottom_new = (bottom + below) * 0.5
    left_rows = jnp.where(
        place == 0, top_new, jnp.where(place == 15, pltpu.roll(bottom_new, 15, 0), left)
    )
    right_rows = jnp.where(
        place == 0, pltpu.roll(top_new, 49, 0), jnp.where(place == 15, bottom_new, right)
    )
    to_east = pltpu.roll(right_rows, 193, 1)
    to_west = pltpu.roll(left_rows, 63, 1)
    src2[0] = jnp.where(half_lane % 64 == 0, to_east[:, :128], pltpu.roll(to_east[:, 128:], 1, 1))
    src2[1] = jnp.where(half_lane % 64 == 63, to_west[:, :128], pltpu.roll(to_west[:, 128:], 1, 1))
    east = remote(src2.at[0], dst2.at[0], send2.at[0], recv2.at[0], (row, (col + 1) % N_COL))
    west = remote(
        src2.at[1], dst2.at[1], send2.at[1], recv2.at[1], (row, (col + N_COL - 1) % N_COL)
    )
    east.start()
    west.start()

    arrived(6)
    for k in range(LEVELS):
        whole = parent_ref[k]
        swapped = jnp.concatenate([whole[128:], whole[:128]], axis=0)
        high, low = split(jnp.where(bits[k] == 0, whole, swapped))
        par_h[k] = high
        par_l[k] = low

    east.wait()
    west.wait()

    def opened(received):
        return jnp.concatenate([received, pltpu.roll(received, 127, 1)], axis=1)

    before = jnp.where(lane % 64 == 0, opened(dst2[0]), pltpu.roll(right_rows, 1, 1))
    after = jnp.where(lane % 64 == 63, opened(dst2[1]), pltpu.roll(left_rows, 255, 1))
    inner = jnp.logical_and(place != 0, place != 15)
    deltas = [
        jnp.where(inner, top_new - top, 0.0),
        jnp.where(inner, bottom_new - bottom, 0.0),
        (left_rows + before) * 0.5 - left,
        (right_rows + after) * 0.5 - right,
    ]
    w = dot3(split(jnp.concatenate(deltas, axis=0)), lift_l)
    k_nodes = k_ref[...].reshape(16, 16, 128)
    k_faces = [k_nodes[0], k_nodes[15], k_nodes[:, 0, :], k_nodes[:, 15, :]]
    skeleton = []
    for f in range(4):
        change = sum(
            w[64 * s + 16 * f : 64 * s + 16 * f + 16] * k_faces[s] for s in range(4)
        )
        skeleton.append(own[f] - jnp.sum(change, axis=0, keepdims=True))
    skeleton = jnp.concatenate(skeleton, axis=0)
    src3[...] = skeleton
    dst3[0] = skeleton
    gathers = []
    for m in range(N_COL - 1, 0, -1):
        slot = bit_reversed(m)
        gathers.append(
            remote(src3, dst3.at[slot], send3.at[m], recv3.at[m], (row, other(m)))
        )
    for copy in gathers:
        copy.start()

    arrived(1, 14)
    solve = split(solve_ref[...])
    face = face_ref[...]
    solve_face = (mm(solve[0], face).astype(BF16), mm(solve[1], face).astype(BF16))
    for f in range(4):
        q = q_ref[256 * f : 256 * f + 256, :].astype(F32)
        change = jnp.concatenate([d[16 * f : 16 * f + 16] for d in deltas], axis=0)
        part_ref[256 * f : 256 * f + 256, :] = dot3(
            solve, split(q - tend_ref[256 * f : 256 * f + 256, :])
        ) - dot3(solve_face, split(change))
    arrived(5, 7, 8)
    chain = None
    interface_maps = []
    for k in range(LEVELS):
        child = split(jnp.where(bits[k] == 0, child_ref[k, :, :128], child_ref[k, :, 128:]))
        sign = (1 - 2 * bits[k]).astype(F32)
        step = mi_ref[k] if chain is None else dot3(split(mi_ref[k]), chain)
        interface_maps.append(step * sign)
        chain = child if chain is None else split(dot3(child, chain))
    interface_map = split(jnp.concatenate(interface_maps, axis=0))
    for part in range(8):
        at = slice(256 * part, 256 * part + 256)
        high, low = split(dot3(split(top_ref[at, :]), chain))
        top_h[at, :] = high
        top_l[at, :] = low
    arrived(11, 9, 10)
    extend = dot3(split(ext_t_ref[...].T), split(spr_e_ref[...]))
    spread_l = split(spr_l_ref[...])

    for copy in gathers:
        copy.wait()
    x = dst3[...].reshape(4 * N_COL, 128)
    differences = []
    for k in range(LEVELS):
        rows = (4 * N_COL) >> (k + 1)
        first, second = x[:rows], x[rows:]
        differences.append((second - first)[:4])
        joined = jnp.concatenate([first, second], axis=1)
        x = dot3(split(joined), (par_h[k], par_l[k]))
    src4[...] = x
    dst4[row] = x
    sends = []
    arrivals = []
    for d in range(1, N_ROW):
        sends.append(remote(src4, dst4.at[row], send4.at[d], recv4.at[d], (row_at(d), col)))
        arrivals.append(
            remote(src4, dst4.at[row_at(N_ROW - d)], send4.at[d], recv4.at[d], (row_at(d), col))
        )
    for copy in sends:
        copy.start()
    boundary = dot3(split(jnp.concatenate(differences, axis=1)), interface_map)
    for copy in sends:
        copy.wait_send()
    for copy in arrivals:
        copy.wait_recv()
    pieces = split(jnp.concatenate([dst4[g] for g in range(N_ROW)], axis=1))
    boundary = boundary + dot3(pieces, (top_h[...], top_l[...]))
    for f in range(4):
        weighted = split(extend * boundary[f : f + 1, :])
        at = slice(256 * f, 256 * f + 256)
        out_ref[at, :] = (part_ref[at, :] + dot3(weighted, spread_l, ((1,), (1,)))).astype(BF16)


def local(
    state_fields, leaf_solve, leaf_flux, lift_edges, lift_leaves, merge_interface, merge_parent,
    split_child, top_inverse, spread_edges, spread_leaves, leaf_extend,
):
    der_h, der_l = derivative_parts()
    dma = pltpu.SemaphoreType.DMA
    args = (
        state_fields.reshape(1024, 256), leaf_solve, leaf_flux, lift_edges, lift_leaves,
        merge_interface, merge_parent, split_child, top_inverse, spread_edges, spread_leaves,
        leaf_extend.T, jnp.asarray(der_h), jnp.asarray(der_l), jnp.asarray(face_columns()),
    )
    result = pl.pallas_call(
        kernel,
        name="imex_step",
        out_shape=jax.ShapeDtypeStruct((1024, 256), BF16),
        in_specs=[pl.BlockSpec(memory_space=pltpu.HBM)] * 15,
        out_specs=pl.BlockSpec(memory_space=pltpu.VMEM),
        scratch_shapes=[pltpu.VMEM(a.shape, a.dtype) for a in args]
        + [
            dma((15,)),
            pltpu.VMEM((1024, 256), F32),
            pltpu.VMEM((1024, 256), F32),
            pltpu.VMEM((256, 128), F32),
            pltpu.VMEM((2, 64, 128), F32),
            pltpu.VMEM((2, 64, 128), F32),
            pltpu.VMEM((2, 64, 128), F32),
            pltpu.VMEM((2, 64, 128), F32),
            pltpu.VMEM((4, 128), F32),
            pltpu.VMEM((N_COL, 4, 128), F32),
            pltpu.VMEM((4, 128), F32),
            pltpu.VMEM((N_ROW, 4, 128), F32),
            pltpu.VMEM((LEVELS, 256, 128), BF16),
            pltpu.VMEM((LEVELS, 256, 128), BF16),
            pltpu.VMEM((2048, 128), BF16),
            pltpu.VMEM((2048, 128), BF16),
            dma((2,)), dma((2,)), dma((2,)), dma((2,)),
            dma((N_COL,)), dma((N_COL,)), dma((N_ROW,)), dma((N_ROW,)),
        ],
        compiler_params=pltpu.CompilerParams(
            collective_id=0, has_side_effects=True, vmem_limit_bytes=67043328
        ),
    )(*args)
    return result.reshape(state_fields.shape)


def solution(mesh):
    in_specs = (
        P(None, None, None, "row", "col", None),
        P(), P(), P(), P(), P(), P(), P(),
        P(None, "row"),
        P(), P(), P(),
    )
    out_specs = P(None, None, None, "row", "col", None)
    return jax.shard_map(local, mesh=mesh, in_specs=in_specs, out_specs=out_specs, check_vma=False)
```

```python
import jax
import jax.numpy as jnp
import numpy as np
from jax import lax
from jax.experimental import pallas as pl
from jax.experimental.pallas import tpu as pltpu
from jax.sharding import PartitionSpec as P

F32 = jnp.float32
BF16 = jnp.bfloat16
MESH = pl.DeviceIdType.MESH
LEVELS = 5
N_ROW = 16
N_COL = 32
advect_scale = 0.01


def chebyshev_matrix(node_count):
    points = np.arange(node_count)
    grid_x = np.cos(np.pi * points / (node_count - 1))
    weights = np.where(points == 0, 2.0, np.where(points == node_count - 1, 2.0, 1.0))
    parity = np.where((points[:, None] + points[None, :]) % 2 == 0, 1.0, -1.0)
    identity = np.eye(node_count)
    spacing = grid_x[:, None] - grid_x[None, :] + identity
    off_diagonal = weights[:, None] / weights[None, :] * parity / spacing * (1.0 - identity)
    result_matrix = off_diagonal - identity * off_diagonal.sum(axis=1)[:, None]
    return result_matrix.astype(np.float32)


def derivative_parts():
    d = chebyshev_matrix(16)
    eye = np.eye(16, dtype=np.float32)
    both = np.concatenate([np.kron(d, eye), np.kron(eye, d)], axis=0) * np.float32(advect_scale)
    high = both.astype(jnp.bfloat16)
    low = (both - high.astype(np.float32)).astype(jnp.bfloat16)
    return high, low


def face_columns():
    e = np.zeros((256, 64), np.float32)
    for k in range(16):
        e[k, k] = 1.0
        e[240 + k, 16 + k] = 1.0
        e[16 * k, 32 + k] = 1.0
        e[16 * k + 15, 48 + k] = 1.0
    return e.astype(jnp.bfloat16)


def split(x):
    high = x.astype(BF16)
    return high, (x - high.astype(F32)).astype(BF16)


def mm(a, b, dims=((1,), (0,))):
    return lax.dot_general(a, b, (dims, ((), ())), preferred_element_type=F32)


def dot3(a, b, dims=((1,), (0,))):
    return mm(a[0], b[0], dims) + mm(a[0], b[1], dims) + mm(a[1], b[0], dims)


def few_rows_dot3(a, b):
    high = a.astype(BF16)
    rows = a.shape[0]
    both = mm(jnp.concatenate([a, a - high.astype(F32)], axis=0).astype(BF16), b[0])
    return both[:rows] + both[rows:] + mm(high, b[1])


def bit_reversed(m):
    return sum(((m >> k) & 1) << (LEVELS - 1 - k) for k in range(LEVELS))


def kernel(*refs):
    stored, out_ref, held, loaded = refs[:15], refs[15], refs[16:31], refs[31]
    step(stored, held, loaded, out_ref, *refs[32:])


def step(
    stored, held, loaded, out_ref,
    tend_ref, part_ref, k_ref, src1, dst1, src2, dst2, src3, dst3, src4, dst4,
    par_h, par_l, top_h, top_l,
    send1, recv1, send2, recv2, send3, recv3, send4, recv4,
):
    row = lax.axis_index("row")
    col = lax.axis_index("col")
    bits = [(col // (1 << k)) % 2 for k in range(LEVELS)]

    def other(m):
        return sum(
            (1 - bits[k] if (m >> k) & 1 else bits[k]) * (1 << k) for k in range(LEVELS)
        )

    def row_at(d):
        return (row + d) % N_ROW

    (
        q_ref, solve_ref, flux_ref, lift_e_ref, lift_l_ref, mi_ref, parent_ref, child_ref,
        top_ref, spr_e_ref, spr_l_ref, ext_t_ref, der_h_ref, der_l_ref, face_ref,
    ) = held
    loads = [
        pltpu.make_async_copy(stored[i], held[i], loaded.at[i]) for i in range(15)
    ]
    for i in (0, 12, 13, 2, 3, 4, 6, 1, 14, 5, 7, 8, 11, 9, 10):
        loads[i].start()

    barrier = pltpu.get_barrier_semaphore()
    for m in range(1, N_COL):
        pl.semaphore_signal(barrier, inc=1, device_id=(row, other(m)), device_id_type=MESH)
    for d in range(1, N_ROW):
        pl.semaphore_signal(barrier, inc=1, device_id=(row_at(d), col), device_id_type=MESH)

    def arrived(*which):
        for i in which:
            loads[i].wait()

    arrived(0, 12, 13)
    der_h, der_l = der_h_ref[...], der_l_ref[...]
    q0 = q_ref[0:256, :].astype(F32)
    q1 = q_ref[256:512, :].astype(F32)
    for f in range(4):
        q = q_ref[256 * f : 256 * f + 256, :]
        both = mm(der_h, q) + mm(der_l, q)
        tend_ref[256 * f : 256 * f + 256, :] = q0 * both[:256] + q1 * both[256:]

    lane = lax.broadcasted_iota(jnp.int32, (64, 256), 1)
    half_lane = lax.broadcasted_iota(jnp.int32, (64, 128), 1)
    place = lax.broadcasted_iota(jnp.int32, (64, 256), 0) % 16

    def rows_of(first):
        return jnp.concatenate(
            [tend_ref[256 * f + first : 256 * f + first + 16, :] for f in range(4)], axis=0
        )

    def nodes_of(first):
        return tend_ref[...].reshape(64, 16, 256)[:, first, :]

    top, bottom = rows_of(0), rows_of(240)
    above = pltpu.roll(bottom, 64, 1)
    below = pltpu.roll(top, 192, 1)
    src1[0] = above[:, :128]
    src1[1] = below[:, 128:]
    pl.semaphore_wait(barrier, N_COL - 1 + N_ROW - 1)

    def remote(src, dst, send, recv, where):
        return pltpu.make_async_remote_copy(
            src_ref=src, dst_ref=dst, send_sem=send, recv_sem=recv, device_id=where,
            device_id_type=MESH,
        )

    south = remote(src1.at[0], dst1.at[0], send1.at[0], recv1.at[0], (row_at(1), col))
    north = remote(src1.at[1], dst1.at[1], send1.at[1], recv1.at[1], (row_at(N_ROW - 1), col))
    south.start()
    north.start()

    arrived(2, 3, 4)
    k_map = dot3(
        split(flux_ref[...].T), split(lift_e_ref[...])
    )
    k_ref[...] = k_map
    lift_l = split(lift_l_ref[...])
    own = []
    for f in range(4):
        q = q_ref[256 * f : 256 * f + 256, :].astype(F32)
        w = dot3(split(q - tend_ref[256 * f : 256 * f + 256, :]), lift_l)
        own.append(jnp.sum(w * k_map, axis=0, keepdims=True))
    left, right = nodes_of(0), nodes_of(15)

    south.wait()
    north.wait()
    above = jnp.where(lane < 64, jnp.concatenate([dst1[0], dst1[0]], axis=1), above)
    below = jnp.where(lane >= 192, jnp.concatenate([dst1[1], dst1[1]], axis=1), below)
    top_new = (top + above) * 0.5
    bottom_new = (bottom + below) * 0.5
    left_rows = jnp.where(
        place == 0, top_new, jnp.where(place == 15, pltpu.roll(bottom_new, 15, 0), left)
    )
    right_rows = jnp.where(
        place == 0, pltpu.roll(top_new, 49, 0), jnp.where(place == 15, bottom_new, right)
    )
    to_east = pltpu.roll(right_rows, 193, 1)
    to_west = pltpu.roll(left_rows, 63, 1)
    src2[0] = jnp.where(half_lane % 64 == 0, to_east[:, :128], pltpu.roll(to_east[:, 128:], 1, 1))
    src2[1] = jnp.where(half_lane % 64 == 63, to_west[:, :128], pltpu.roll(to_west[:, 128:], 1, 1))
    east = remote(src2.at[0], dst2.at[0], send2.at[0], recv2.at[0], (row, (col + 1) % N_COL))
    west = remote(
        src2.at[1], dst2.at[1], send2.at[1], recv2.at[1], (row, (col + N_COL - 1) % N_COL)
    )
    east.start()
    west.start()

    arrived(6)
    for k in range(LEVELS):
        whole = parent_ref[k]
        swapped = jnp.concatenate([whole[128:], whole[:128]], axis=0)
        high, low = split(jnp.where(bits[k] == 0, whole, swapped))
        par_h[k] = high
        par_l[k] = low

    east.wait()
    west.wait()

    def opened(received):
        return jnp.concatenate([received, pltpu.roll(received, 127, 1)], axis=1)

    before = jnp.where(lane % 64 == 0, opened(dst2[0]), pltpu.roll(right_rows, 1, 1))
    after = jnp.where(lane % 64 == 63, opened(dst2[1]), pltpu.roll(left_rows, 255, 1))
    inner = jnp.logical_and(place != 0, place != 15)
    deltas = [
        jnp.where(inner, top_new - top, 0.0),
        jnp.where(inner, bottom_new - bottom, 0.0),
        (left_rows + before) * 0.5 - left,
        (right_rows + after) * 0.5 - right,
    ]
    w = dot3(split(jnp.concatenate(deltas, axis=0)), lift_l)
    k_nodes = k_ref[...].reshape(16, 16, 128)
    k_faces = [k_nodes[0], k_nodes[15], k_nodes[:, 0, :], k_nodes[:, 15, :]]
    skeleton = []
    for f in range(4):
        change = sum(
            w[64 * s + 16 * f : 64 * s + 16 * f + 16] * k_faces[s] for s in range(4)
        )
        skeleton.append(own[f] - jnp.sum(change, axis=0, keepdims=True))
    skeleton = jnp.concatenate(skeleton, axis=0)
    src3[...] = skeleton
    dst3[0] = skeleton
    gathers = []
    for m in range(N_COL - 1, 0, -1):
        slot = bit_reversed(m)
        gathers.append(
            remote(src3, dst3.at[slot], send3.at[m], recv3.at[m], (row, other(m)))
        )
    for copy in gathers:
        copy.start()

    arrived(1, 14)
    solve = split(solve_ref[...])
    face = face_ref[...]
    solve_face = (mm(solve[0], face).astype(BF16), mm(solve[1], face).astype(BF16))
    for f in range(4):
        q = q_ref[256 * f : 256 * f + 256, :].astype(F32)
        change = jnp.concatenate([d[16 * f : 16 * f + 16] for d in deltas], axis=0)
        part_ref[256 * f : 256 * f + 256, :] = dot3(
            solve, split(q - tend_ref[256 * f : 256 * f + 256, :])
        ) - dot3(solve_face, split(change))
    arrived(5, 7, 8)
    chain = None
    interface_maps = []
    for k in range(LEVELS):
        child = split(jnp.where(bits[k] == 0, child_ref[k, :, :128], child_ref[k, :, 128:]))
        sign = (1 - 2 * bits[k]).astype(F32)
        step = mi_ref[k] if chain is None else dot3(split(mi_ref[k]), chain)
        interface_maps.append(step * sign)
        chain = child if chain is None else split(dot3(child, chain))
    interface_map = split(jnp.concatenate(interface_maps, axis=0))
    for part in range(8):
        at = slice(256 * part, 256 * part + 256)
        high, low = split(dot3(split(top_ref[at, :]), chain))
        top_h[at, :] = high
        top_l[at, :] = low
    arrived(11, 9, 10)
    extend = dot3(split(ext_t_ref[...].T), split(spr_e_ref[...]))
    spread_h, spread_low = split(spr_l_ref[...])
    spread_twice = jnp.concatenate([spread_h, spread_h], axis=1)

    for copy in gathers:
        copy.wait_recv()
    x = dst3[...].reshape(4 * N_COL, 128)
    differences = []
    for k in range(LEVELS):
        rows = (4 * N_COL) >> (k + 1)
        first, second = x[:rows], x[rows:]
        differences.append((second - first)[:4])
        joined = jnp.concatenate([first, second], axis=1)
        x = few_rows_dot3(joined, (par_h[k], par_l[k]))
    src4[...] = x
    dst4[row] = x
    sends = []
    arrivals = []
    for d in range(1, N_ROW):
        sends.append(remote(src4, dst4.at[row], send4.at[d], recv4.at[d], (row_at(d), col)))
        arrivals.append(
            remote(src4, dst4.at[row_at(N_ROW - d)], send4.at[d], recv4.at[d], (row_at(d), col))
        )
    for copy in sends:
        copy.start()
    boundary = few_rows_dot3(jnp.concatenate(differences, axis=1), interface_map)
    for copy in gathers + sends:
        copy.wait_send()
    for copy in arrivals:
        copy.wait_recv()
    pieces = jnp.concatenate([dst4[g] for g in range(N_ROW)], axis=1)
    boundary = boundary + few_rows_dot3(pieces, (top_h[...], top_l[...]))
    for f in range(4):
        weighted = split(extend * boundary[f : f + 1, :])
        at = slice(256 * f, 256 * f + 256)
        edges = mm(jnp.concatenate(weighted, axis=1), spread_twice, ((1,), (1,)))
        edges = edges + mm(weighted[0], spread_low, ((1,), (1,)))
        out_ref[at, :] = (part_ref[at, :] + edges).astype(BF16)


def local(
    state_fields, leaf_solve, leaf_flux, lift_edges, lift_leaves, merge_interface, merge_parent,
    split_child, top_inverse, spread_edges, spread_leaves, leaf_extend,
):
    der_h, der_l = derivative_parts()
    dma = pltpu.SemaphoreType.DMA
    args = (
        state_fields.reshape(1024, 256), leaf_solve, leaf_flux, lift_edges, lift_leaves,
        merge_interface, merge_parent, split_child, top_inverse, spread_edges, spread_leaves,
        leaf_extend.T, jnp.asarray(der_h), jnp.asarray(der_l), jnp.asarray(face_columns()),
    )
    result = pl.pallas_call(
        kernel,
        name="imex_step",
        out_shape=jax.ShapeDtypeStruct((1024, 256), BF16),
        in_specs=[pl.BlockSpec(memory_space=pltpu.HBM)] * 15,
        out_specs=pl.BlockSpec(memory_space=pltpu.VMEM),
        scratch_shapes=[pltpu.VMEM(a.shape, a.dtype) for a in args]
        + [
            dma((15,)),
            pltpu.VMEM((1024, 256), F32),
            pltpu.VMEM((1024, 256), F32),
            pltpu.VMEM((256, 128), F32),
            pltpu.VMEM((2, 64, 128), F32),
            pltpu.VMEM((2, 64, 128), F32),
            pltpu.VMEM((2, 64, 128), F32),
            pltpu.VMEM((2, 64, 128), F32),
            pltpu.VMEM((4, 128), F32),
            pltpu.VMEM((N_COL, 4, 128), F32),
            pltpu.VMEM((4, 128), F32),
            pltpu.VMEM((N_ROW, 4, 128), F32),
            pltpu.VMEM((LEVELS, 256, 128), BF16),
            pltpu.VMEM((LEVELS, 256, 128), BF16),
            pltpu.VMEM((2048, 128), BF16),
            pltpu.VMEM((2048, 128), BF16),
            dma((2,)), dma((2,)), dma((2,)), dma((2,)),
            dma((N_COL,)), dma((N_COL,)), dma((N_ROW,)), dma((N_ROW,)),
        ],
        compiler_params=pltpu.CompilerParams(
            collective_id=0, has_side_effects=True, vmem_limit_bytes=48 * 1024 * 1024
        ),
    )(*[pltpu.with_memory_space_constraint(a, pltpu.HBM) for a in args])
    return result.reshape(state_fields.shape)


def solution(mesh):
    in_specs = (
        P(None, None, None, "row", "col", None),
        P(), P(), P(), P(), P(), P(), P(),
        P(None, "row"),
        P(), P(), P(),
    )
    out_specs = P(None, None, None, "row", "col", None)
    return jax.shard_map(local, mesh=mesh, in_specs=in_specs, out_specs=out_specs, check_vma=False)
```

```python
import jax
import jax.numpy as jnp
import numpy as np
from jax import lax
from jax.experimental import pallas as pl
from jax.experimental.pallas import tpu as pltpu
from jax.sharding import PartitionSpec as P

F32 = jnp.float32
BF16 = jnp.bfloat16
MESH = pl.DeviceIdType.MESH
LEVELS = 5
N_ROW = 16
N_COL = 32
LOW = 3
HIGH = LEVELS - LOW
NEAR = [m for m in range(7, 0, -1)]
FAR = [m << LOW for m in range(3, 0, -1)]
advect_scale = 0.01


def chebyshev_matrix(node_count):
    points = np.arange(node_count)
    grid_x = np.cos(np.pi * points / (node_count - 1))
    weights = np.where(points == 0, 2.0, np.where(points == node_count - 1, 2.0, 1.0))
    parity = np.where((points[:, None] + points[None, :]) % 2 == 0, 1.0, -1.0)
    identity = np.eye(node_count)
    spacing = grid_x[:, None] - grid_x[None, :] + identity
    off_diagonal = weights[:, None] / weights[None, :] * parity / spacing * (1.0 - identity)
    result_matrix = off_diagonal - identity * off_diagonal.sum(axis=1)[:, None]
    return result_matrix.astype(np.float32)


def derivative_parts():
    d = chebyshev_matrix(16)
    eye = np.eye(16, dtype=np.float32)
    both = np.concatenate([np.kron(d, eye), np.kron(eye, d)], axis=0) * np.float32(advect_scale)
    high = both.astype(jnp.bfloat16)
    low = (both - high.astype(np.float32)).astype(jnp.bfloat16)
    return high, low


def face_columns():
    e = np.zeros((256, 64), np.float32)
    for k in range(16):
        e[k, k] = 1.0
        e[240 + k, 16 + k] = 1.0
        e[16 * k, 32 + k] = 1.0
        e[16 * k + 15, 48 + k] = 1.0
    return e.astype(jnp.bfloat16)


def split(x):
    high = x.astype(BF16)
    return high, (x - high.astype(F32)).astype(BF16)


def mm(a, b, dims=((1,), (0,))):
    return lax.dot_general(a, b, (dims, ((), ())), preferred_element_type=F32)


def dot3(a, b, dims=((1,), (0,))):
    return mm(a[0], b[0], dims) + mm(a[0], b[1], dims) + mm(a[1], b[0], dims)


def few_rows_dot3(a, b):
    high = a.astype(BF16)
    rows = a.shape[0]
    both = mm(jnp.concatenate([a, a - high.astype(F32)], axis=0).astype(BF16), b[0])
    return both[:rows] + both[rows:] + mm(high, b[1])


def bit_reversed(m, width):
    return sum(((m >> k) & 1) << (width - 1 - k) for k in range(width))


def kernel(*refs):
    stored, out_ref, held, loaded = refs[:15], refs[15], refs[16:31], refs[31]
    step(stored, held, loaded, out_ref, *refs[32:])


def step(
    stored, held, loaded, out_ref,
    tend_ref, part_ref, k_ref, src1, dst1, src2, dst2, src3, dst3, src4, dst4, src5, dst5,
    par_h, par_l, top_h, top_l,
    send1, recv1, send2, recv2, send3, recv3, send4, recv4, send5, recv5,
):
    row = lax.axis_index("row")
    col = lax.axis_index("col")
    bits = [(col // (1 << k)) % 2 for k in range(LEVELS)]

    def other(m):
        return sum(
            (1 - bits[k] if (m >> k) & 1 else bits[k]) * (1 << k) for k in range(LEVELS)
        )

    def row_at(d):
        return (row + d) % N_ROW

    (
        q_ref, solve_ref, flux_ref, lift_e_ref, lift_l_ref, mi_ref, parent_ref, child_ref,
        top_ref, spr_e_ref, spr_l_ref, ext_t_ref, der_h_ref, der_l_ref, face_ref,
    ) = held
    loads = [
        pltpu.make_async_copy(stored[i], held[i], loaded.at[i]) for i in range(15)
    ]
    for i in (0, 12, 13, 2, 3, 4, 6, 1, 14, 5, 7, 8, 11, 9, 10):
        loads[i].start()

    barrier = pltpu.get_barrier_semaphore()
    peers = [(row_at(d), col) for d in (8, 7, 9, 6, 10, 5, 11, 4, 12, 3, 13, 2, 14, 1, 15)]
    peers += [(row, other(m)) for m in NEAR + FAR]
    peers += [(row, (col + 1) % N_COL), (row, (col + N_COL - 1) % N_COL)]
    for peer in peers:
        pl.semaphore_signal(barrier, inc=1, device_id=peer, device_id_type=MESH)

    def arrived(*which):
        for i in which:
            loads[i].wait()

    arrived(0, 12, 13)
    der_h, der_l = der_h_ref[...], der_l_ref[...]
    q0 = q_ref[0:256, :].astype(F32)
    q1 = q_ref[256:512, :].astype(F32)
    for f in range(4):
        q = q_ref[256 * f : 256 * f + 256, :]
        both = mm(der_h, q) + mm(der_l, q)
        tend_ref[256 * f : 256 * f + 256, :] = q0 * both[:256] + q1 * both[256:]

    lane = lax.broadcasted_iota(jnp.int32, (64, 256), 1)
    half_lane = lax.broadcasted_iota(jnp.int32, (64, 128), 1)
    place = lax.broadcasted_iota(jnp.int32, (64, 256), 0) % 16

    def rows_of(first):
        return jnp.concatenate(
            [tend_ref[256 * f + first : 256 * f + first + 16, :] for f in range(4)], axis=0
        )

    def nodes_of(first):
        return tend_ref[...].reshape(64, 16, 256)[:, first, :]

    top, bottom = rows_of(0), rows_of(240)
    above = pltpu.roll(bottom, 64, 1)
    below = pltpu.roll(top, 192, 1)
    src1[0] = above[:, :128]
    src1[1] = below[:, 128:]
    pl.semaphore_wait(barrier, len(peers))

    def remote(src, dst, send, recv, where):
        return pltpu.make_async_remote_copy(
            src_ref=src, dst_ref=dst, send_sem=send, recv_sem=recv, device_id=where,
            device_id_type=MESH,
        )

    south = remote(src1.at[0], dst1.at[0], send1.at[0], recv1.at[0], (row_at(1), col))
    north = remote(src1.at[1], dst1.at[1], send1.at[1], recv1.at[1], (row_at(N_ROW - 1), col))
    south.start()
    north.start()

    arrived(2, 3, 4)
    k_map = dot3(
        split(flux_ref[...].T), split(lift_e_ref[...])
    )
    k_ref[...] = k_map
    lift_l = split(lift_l_ref[...])
    own = []
    for f in range(4):
        q = q_ref[256 * f : 256 * f + 256, :].astype(F32)
        w = dot3(split(q - tend_ref[256 * f : 256 * f + 256, :]), lift_l)
        own.append(jnp.sum(w * k_map, axis=0, keepdims=True))
    left, right = nodes_of(0), nodes_of(15)

    south.wait()
    north.wait()
    above = jnp.where(lane < 64, jnp.concatenate([dst1[0], dst1[0]], axis=1), above)
    below = jnp.where(lane >= 192, jnp.concatenate([dst1[1], dst1[1]], axis=1), below)
    top_new = (top + above) * 0.5
    bottom_new = (bottom + below) * 0.5
    left_rows = jnp.where(
        place == 0, top_new, jnp.where(place == 15, pltpu.roll(bottom_new, 15, 0), left)
    )
    right_rows = jnp.where(
        place == 0, pltpu.roll(top_new, 49, 0), jnp.where(place == 15, bottom_new, right)
    )
    to_east = pltpu.roll(right_rows, 193, 1)
    to_west = pltpu.roll(left_rows, 63, 1)
    src2[0] = jnp.where(half_lane % 64 == 0, to_east[:, :128], pltpu.roll(to_east[:, 128:], 1, 1))
    src2[1] = jnp.where(half_lane % 64 == 63, to_west[:, :128], pltpu.roll(to_west[:, 128:], 1, 1))
    east = remote(src2.at[0], dst2.at[0], send2.at[0], recv2.at[0], (row, (col + 1) % N_COL))
    west = remote(
        src2.at[1], dst2.at[1], send2.at[1], recv2.at[1], (row, (col + N_COL - 1) % N_COL)
    )
    east.start()
    west.start()

    arrived(6)
    for k in range(LEVELS):
        whole = parent_ref[k]
        swapped = jnp.concatenate([whole[128:], whole[:128]], axis=0)
        high, low = split(jnp.where(bits[k] == 0, whole, swapped))
        par_h[k] = high
        par_l[k] = low

    east.wait()
    west.wait()

    def opened(received):
        return jnp.concatenate([received, pltpu.roll(received, 127, 1)], axis=1)

    before = jnp.where(lane % 64 == 0, opened(dst2[0]), pltpu.roll(right_rows, 1, 1))
    after = jnp.where(lane % 64 == 63, opened(dst2[1]), pltpu.roll(left_rows, 255, 1))
    inner = jnp.logical_and(place != 0, place != 15)
    deltas = [
        jnp.where(inner, top_new - top, 0.0),
        jnp.where(inner, bottom_new - bottom, 0.0),
        (left_rows + before) * 0.5 - left,
        (right_rows + after) * 0.5 - right,
    ]
    w = dot3(split(jnp.concatenate(deltas, axis=0)), lift_l)
    k_nodes = k_ref[...].reshape(16, 16, 128)
    k_faces = [k_nodes[0], k_nodes[15], k_nodes[:, 0, :], k_nodes[:, 15, :]]
    skeleton = []
    for f in range(4):
        change = sum(
            w[64 * s + 16 * f : 64 * s + 16 * f + 16] * k_faces[s] for s in range(4)
        )
        skeleton.append(own[f] - jnp.sum(change, axis=0, keepdims=True))
    skeleton = jnp.concatenate(skeleton, axis=0)
    src3[...] = skeleton
    dst3[0] = skeleton
    gathers = [
        remote(src3, dst3.at[bit_reversed(m, LOW)], send3.at[m], recv3.at[m], (row, other(m)))
        for m in NEAR
    ]
    for copy in gathers:
        copy.start()

    arrived(1, 14)
    solve = split(solve_ref[...])
    face = face_ref[...]
    solve_face = (mm(solve[0], face).astype(BF16), mm(solve[1], face).astype(BF16))
    for f in range(4):
        q = q_ref[256 * f : 256 * f + 256, :].astype(F32)
        change = jnp.concatenate([d[16 * f : 16 * f + 16] for d in deltas], axis=0)
        part_ref[256 * f : 256 * f + 256, :] = dot3(
            solve, split(q - tend_ref[256 * f : 256 * f + 256, :])
        ) - dot3(solve_face, split(change))
    for copy in gathers:
        copy.wait_recv()
    differences = []

    def merged(x, level):
        rows = x.shape[0] // 2
        first, second = x[:rows], x[rows:]
        differences.append((second - first)[:4])
        joined = jnp.concatenate([first, second], axis=1)
        return few_rows_dot3(joined, (par_h[level], par_l[level]))

    x = dst3[...].reshape(4 << LOW, 128)
    for k in range(LOW):
        x = merged(x, k)
    src5[...] = x
    dst5[0] = x
    crossings = [
        remote(
            src5, dst5.at[bit_reversed(m >> LOW, HIGH)], send5.at[m >> LOW], recv5.at[m >> LOW],
            (row, other(m)),
        )
        for m in FAR
    ]
    for copy in crossings:
        copy.start()

    arrived(5, 7, 8)
    chain = None
    interface_maps = []
    for k in range(LEVELS):
        child = split(jnp.where(bits[k] == 0, child_ref[k, :, :128], child_ref[k, :, 128:]))
        sign = (1 - 2 * bits[k]).astype(F32)
        step = mi_ref[k] if chain is None else dot3(split(mi_ref[k]), chain)
        interface_maps.append(step * sign)
        chain = child if chain is None else split(dot3(child, chain))
    interface_map = split(jnp.concatenate(interface_maps, axis=0))
    for part in range(8):
        at = slice(256 * part, 256 * part + 256)
        high, low = split(dot3(split(top_ref[at, :]), chain))
        top_h[at, :] = high
        top_l[at, :] = low
    arrived(11, 9, 10)
    extend = dot3(split(ext_t_ref[...].T), split(spr_e_ref[...]))
    spread_h, spread_low = split(spr_l_ref[...])
    spread_twice = jnp.concatenate([spread_h, spread_h], axis=1)

    for copy in crossings:
        copy.wait_recv()
    x = dst5[...].reshape(4 << HIGH, 128)
    for k in range(LOW, LEVELS):
        x = merged(x, k)
    src4[...] = x
    dst4[row] = x
    sends = []
    arrivals = []
    for d in range(1, N_ROW):
        sends.append(remote(src4, dst4.at[row], send4.at[d], recv4.at[d], (row_at(d), col)))
        arrivals.append(
            remote(src4, dst4.at[row_at(N_ROW - d)], send4.at[d], recv4.at[d], (row_at(d), col))
        )
    for copy in sends:
        copy.start()
    boundary = few_rows_dot3(jnp.concatenate(differences, axis=1), interface_map)
    for copy in gathers + crossings + sends:
        copy.wait_send()
    for copy in arrivals:
        copy.wait_recv()
    pieces = jnp.concatenate([dst4[g] for g in range(N_ROW)], axis=1)
    boundary = boundary + few_rows_dot3(pieces, (top_h[...], top_l[...]))
    for f in range(4):
        weighted = split(extend * boundary[f : f + 1, :])
        at = slice(256 * f, 256 * f + 256)
        edges = mm(jnp.concatenate(weighted, axis=1), spread_twice, ((1,), (1,)))
        edges = edges + mm(weighted[0], spread_low, ((1,), (1,)))
        out_ref[at, :] = (part_ref[at, :] + edges).astype(BF16)


def local(
    state_fields, leaf_solve, leaf_flux, lift_edges, lift_leaves, merge_interface, merge_parent,
    split_child, top_inverse, spread_edges, spread_leaves, leaf_extend,
):
    der_h, der_l = derivative_parts()
    dma = pltpu.SemaphoreType.DMA
    args = (
        state_fields.reshape(1024, 256), leaf_solve, leaf_flux, lift_edges, lift_leaves,
        merge_interface, merge_parent, split_child, top_inverse, spread_edges, spread_leaves,
        leaf_extend.T, jnp.asarray(der_h), jnp.asarray(der_l), jnp.asarray(face_columns()),
    )
    result = pl.pallas_call(
        kernel,
        name="imex_step",
        out_shape=jax.ShapeDtypeStruct((1024, 256), BF16),
        in_specs=[pl.BlockSpec(memory_space=pltpu.HBM)] * 15,
        out_specs=pl.BlockSpec(memory_space=pltpu.VMEM),
        scratch_shapes=[pltpu.VMEM(a.shape, a.dtype) for a in args]
        + [
            dma((15,)),
            pltpu.VMEM((1024, 256), F32),
            pltpu.VMEM((1024, 256), F32),
            pltpu.VMEM((256, 128), F32),
            pltpu.VMEM((2, 64, 128), F32),
            pltpu.VMEM((2, 64, 128), F32),
            pltpu.VMEM((2, 64, 128), F32),
            pltpu.VMEM((2, 64, 128), F32),
            pltpu.VMEM((4, 128), F32),
            pltpu.VMEM((1 << LOW, 4, 128), F32),
            pltpu.VMEM((4, 128), F32),
            pltpu.VMEM((N_ROW, 4, 128), F32),
            pltpu.VMEM((4, 128), F32),
            pltpu.VMEM((1 << HIGH, 4, 128), F32),
            pltpu.VMEM((LEVELS, 256, 128), BF16),
            pltpu.VMEM((LEVELS, 256, 128), BF16),
            pltpu.VMEM((2048, 128), BF16),
            pltpu.VMEM((2048, 128), BF16),
            dma((2,)), dma((2,)), dma((2,)), dma((2,)),
            dma((1 << LOW,)), dma((1 << LOW,)), dma((N_ROW,)), dma((N_ROW,)),
            dma((1 << HIGH,)), dma((1 << HIGH,)),
        ],
        compiler_params=pltpu.CompilerParams(
            collective_id=0, has_side_effects=True, vmem_limit_bytes=48 * 1024 * 1024
        ),
    )(*[pltpu.with_memory_space_constraint(a, pltpu.HBM) for a in args])
    return result.reshape(state_fields.shape)


def solution(mesh):
    in_specs = (
        P(None, None, None, "row", "col", None),
        P(), P(), P(), P(), P(), P(), P(),
        P(None, "row"),
        P(), P(), P(),
    )
    out_specs = P(None, None, None, "row", "col", None)
    return jax.shard_map(local, mesh=mesh, in_specs=in_specs, out_specs=out_specs, check_vma=False)
```

```python
import jax
import jax.numpy as jnp
import numpy as np
from jax import lax
from jax.experimental import pallas as pl
from jax.experimental.pallas import tpu as pltpu
from jax.sharding import PartitionSpec as P

F32 = jnp.float32
BF16 = jnp.bfloat16
MESH = pl.DeviceIdType.MESH
LEVELS = 5
N_ROW = 16
N_COL = 32
advect_scale = 0.01


def chebyshev_matrix(node_count):
    points = np.arange(node_count)
    grid_x = np.cos(np.pi * points / (node_count - 1))
    weights = np.where(points == 0, 2.0, np.where(points == node_count - 1, 2.0, 1.0))
    parity = np.where((points[:, None] + points[None, :]) % 2 == 0, 1.0, -1.0)
    identity = np.eye(node_count)
    spacing = grid_x[:, None] - grid_x[None, :] + identity
    off_diagonal = weights[:, None] / weights[None, :] * parity / spacing * (1.0 - identity)
    result_matrix = off_diagonal - identity * off_diagonal.sum(axis=1)[:, None]
    return result_matrix.astype(np.float32)


def derivative_parts():
    d = chebyshev_matrix(16)
    eye = np.eye(16, dtype=np.float32)
    both = np.concatenate([np.kron(d, eye), np.kron(eye, d)], axis=0) * np.float32(advect_scale)
    high = both.astype(jnp.bfloat16)
    low = (both - high.astype(np.float32)).astype(jnp.bfloat16)
    return high, low


def face_columns():
    e = np.zeros((256, 64), np.float32)
    for k in range(16):
        e[k, k] = 1.0
        e[240 + k, 16 + k] = 1.0
        e[16 * k, 32 + k] = 1.0
        e[16 * k + 15, 48 + k] = 1.0
    return e.astype(jnp.bfloat16)


def split(x):
    high = x.astype(BF16)
    return high, (x - high.astype(F32)).astype(BF16)


def mm(a, b, dims=((1,), (0,))):
    return lax.dot_general(a, b, (dims, ((), ())), preferred_element_type=F32)


def dot3(a, b, dims=((1,), (0,))):
    return mm(a[0], b[0], dims) + mm(a[0], b[1], dims) + mm(a[1], b[0], dims)


def few_rows_dot3(a, b):
    high = a.astype(BF16)
    rows = a.shape[0]
    both = mm(jnp.concatenate([a, a - high.astype(F32)], axis=0).astype(BF16), b[0])
    return both[:rows] + both[rows:] + mm(high, b[1])


def bit_reversed(m):
    return sum(((m >> k) & 1) << (LEVELS - 1 - k) for k in range(LEVELS))


def kernel(*refs):
    stored, out_ref, held, loaded = refs[:15], refs[15], refs[16:31], refs[31]
    step(stored, held, loaded, out_ref, *refs[32:])


def step(
    stored, held, loaded, out_ref,
    tend_ref, part_ref, k_ref, src1, dst1, src2, dst2, src3, dst3, src4, dst4, src6, dst6,
    par_h, par_l, top_h, top_l,
    send1, recv1, send2, recv2, send3, recv3, send4, recv4, send6, recv6,
):
    row = lax.axis_index("row")
    col = lax.axis_index("col")
    bits = [(col // (1 << k)) % 2 for k in range(LEVELS)]

    def other(m):
        return sum(
            (1 - bits[k] if (m >> k) & 1 else bits[k]) * (1 << k) for k in range(LEVELS)
        )

    def row_at(d):
        return (row + d) % N_ROW

    (
        q_ref, solve_ref, flux_ref, lift_e_ref, lift_l_ref, mi_ref, parent_ref, child_ref,
        top_ref, spr_e_ref, spr_l_ref, ext_t_ref, der_h_ref, der_l_ref, face_ref,
    ) = held
    loads = [
        pltpu.make_async_copy(stored[i], held[i], loaded.at[i]) for i in range(15)
    ]
    for i in (0, 12, 13, 2, 3, 4, 6, 1, 14, 5, 7, 8, 11, 9, 10):
        loads[i].start()

    barrier = pltpu.get_barrier_semaphore()
    for m in range(1, N_COL):
        pl.semaphore_signal(barrier, inc=1, device_id=(row, other(m)), device_id_type=MESH)
    for d in range(1, N_ROW):
        pl.semaphore_signal(barrier, inc=1, device_id=(row_at(d), col), device_id_type=MESH)
    down, up = row_at(1), row_at(N_ROW - 1)
    east_col, west_col = (col + 1) % N_COL, (col + N_COL - 1) % N_COL
    diagonal = [(down, east_col), (down, west_col), (up, east_col), (up, west_col)]
    for peer in diagonal:
        pl.semaphore_signal(barrier, inc=1, device_id=peer, device_id_type=MESH)

    def arrived(*which):
        for i in which:
            loads[i].wait()

    arrived(0, 12, 13)
    der_h, der_l = der_h_ref[...], der_l_ref[...]
    q0 = q_ref[0:256, :].astype(F32)
    q1 = q_ref[256:512, :].astype(F32)
    for f in range(4):
        q = q_ref[256 * f : 256 * f + 256, :]
        both = mm(der_h, q) + mm(der_l, q)
        tend_ref[256 * f : 256 * f + 256, :] = q0 * both[:256] + q1 * both[256:]

    lane = lax.broadcasted_iota(jnp.int32, (64, 256), 1)
    half_lane = lax.broadcasted_iota(jnp.int32, (64, 128), 1)
    place = lax.broadcasted_iota(jnp.int32, (64, 256), 0) % 16

    def rows_of(first):
        return jnp.concatenate(
            [tend_ref[256 * f + first : 256 * f + first + 16, :] for f in range(4)], axis=0
        )

    def nodes_of(first):
        return tend_ref[...].reshape(64, 16, 256)[:, first, :]

    top, bottom = rows_of(0), rows_of(240)
    above = pltpu.roll(bottom, 64, 1)
    below = pltpu.roll(top, 192, 1)
    src1[0] = above[:, :128]
    src1[1] = below[:, 128:]

    left, right = nodes_of(0), nodes_of(15)

    def with_corners(top_rows, bottom_rows):
        left_rows = jnp.where(
            place == 0, top_rows, jnp.where(place == 15, pltpu.roll(bottom_rows, 15, 0), left)
        )
        right_rows = jnp.where(
            place == 0, pltpu.roll(top_rows, 49, 0), jnp.where(place == 15, bottom_rows, right)
        )
        return left_rows, right_rows

    left_part, right_part = with_corners(
        (top + jnp.where(lane < 64, 0.0, above)) * 0.5,
        (bottom + jnp.where(lane >= 192, 0.0, below)) * 0.5,
    )
    to_east = pltpu.roll(right_part, 193, 1)
    to_west = pltpu.roll(left_part, 63, 1)
    src2[0] = jnp.where(half_lane % 64 == 0, to_east[:, :128], pltpu.roll(to_east[:, 128:], 1, 1))
    src2[1] = jnp.where(half_lane % 64 == 63, to_west[:, :128], pltpu.roll(to_west[:, 128:], 1, 1))

    def corner(rows, shift, node):
        return pltpu.roll(rows, shift, 1).reshape(4, 16, 128)[:, node, :]

    src6[0] = corner(above[:, :128], 65, 15)
    src6[1] = corner(above[:, :128], 63, 0)
    src6[2] = corner(below[:, 128:], 65, 15)
    src6[3] = corner(below[:, 128:], 63, 0)
    pl.semaphore_wait(barrier, N_COL - 1 + N_ROW - 1 + 4)

    def remote(src, dst, send, recv, where):
        return pltpu.make_async_remote_copy(
            src_ref=src, dst_ref=dst, send_sem=send, recv_sem=recv, device_id=where,
            device_id_type=MESH,
        )

    faces = [
        remote(src6.at[k], dst6.at[k], send6.at[k], recv6.at[k], diagonal[k]) for k in range(4)
    ]
    faces += [
        remote(src2.at[0], dst2.at[0], send2.at[0], recv2.at[0], (row, east_col)),
        remote(src2.at[1], dst2.at[1], send2.at[1], recv2.at[1], (row, west_col)),
        remote(src1.at[0], dst1.at[0], send1.at[0], recv1.at[0], (down, col)),
        remote(src1.at[1], dst1.at[1], send1.at[1], recv1.at[1], (up, col)),
    ]
    for copy in faces:
        copy.start()

    arrived(2, 3, 4)
    k_map = dot3(
        split(flux_ref[...].T), split(lift_e_ref[...])
    )
    k_ref[...] = k_map
    lift_l = split(lift_l_ref[...])
    own = []
    for f in range(4):
        q = q_ref[256 * f : 256 * f + 256, :].astype(F32)
        w = dot3(split(q - tend_ref[256 * f : 256 * f + 256, :]), lift_l)
        own.append(jnp.sum(w * k_map, axis=0, keepdims=True))
    arrived(6)
    for k in range(LEVELS):
        whole = parent_ref[k]
        swapped = jnp.concatenate([whole[128:], whole[:128]], axis=0)
        high, low = split(jnp.where(bits[k] == 0, whole, swapped))
        par_h[k] = high
        par_l[k] = low

    for copy in faces:
        copy.wait()
    above = jnp.where(lane < 64, jnp.concatenate([dst1[0], dst1[0]], axis=1), above)
    below = jnp.where(lane >= 192, jnp.concatenate([dst1[1], dst1[1]], axis=1), below)
    top_new = (top + above) * 0.5
    bottom_new = (bottom + below) * 0.5
    left_rows, right_rows = with_corners(top_new, bottom_new)

    def opened(received):
        return jnp.concatenate([received, pltpu.roll(received, 127, 1)], axis=1)

    def spread_corner(k, node, at):
        rows = dst6[k]
        rows = jnp.concatenate(
            [jnp.broadcast_to(rows[f : f + 1], (16, 128)) for f in range(4)], axis=0
        )
        here = jnp.logical_and(place == node, lane == at)
        return jnp.where(here, jnp.concatenate([rows, rows], axis=1) * 0.5, 0.0)

    before = jnp.where(lane % 64 == 0, opened(dst2[0]), pltpu.roll(right_rows, 1, 1))
    before = before + spread_corner(0, 0, 0) + spread_corner(2, 15, 192)
    after = jnp.where(lane % 64 == 63, opened(dst2[1]), pltpu.roll(left_rows, 255, 1))
    after = after + spread_corner(1, 0, 63) + spread_corner(3, 15, 255)
    inner = jnp.logical_and(place != 0, place != 15)
    deltas = [
        jnp.where(inner, top_new - top, 0.0),
        jnp.where(inner, bottom_new - bottom, 0.0),
        (left_rows + before) * 0.5 - left,
        (right_rows + after) * 0.5 - right,
    ]
    w = dot3(split(jnp.concatenate(deltas, axis=0)), lift_l)
    k_nodes = k_ref[...].reshape(16, 16, 128)
    k_faces = [k_nodes[0], k_nodes[15], k_nodes[:, 0, :], k_nodes[:, 15, :]]
    skeleton = []
    for f in range(4):
        change = sum(
            w[64 * s + 16 * f : 64 * s + 16 * f + 16] * k_faces[s] for s in range(4)
        )
        skeleton.append(own[f] - jnp.sum(change, axis=0, keepdims=True))
    skeleton = jnp.concatenate(skeleton, axis=0)
    src3[...] = skeleton
    dst3[0] = skeleton
    gathers = []
    for m in range(N_COL - 1, 0, -1):
        slot = bit_reversed(m)
        gathers.append(
            remote(src3, dst3.at[slot], send3.at[m], recv3.at[m], (row, other(m)))
        )
    for copy in gathers:
        copy.start()

    arrived(1, 14)
    solve = split(solve_ref[...])
    face = face_ref[...]
    solve_face = (mm(solve[0], face).astype(BF16), mm(solve[1], face).astype(BF16))
    for f in range(4):
        q = q_ref[256 * f : 256 * f + 256, :].astype(F32)
        change = jnp.concatenate([d[16 * f : 16 * f + 16] for d in deltas], axis=0)
        part_ref[256 * f : 256 * f + 256, :] = dot3(
            solve, split(q - tend_ref[256 * f : 256 * f + 256, :])
        ) - dot3(solve_face, split(change))
    arrived(5, 7, 8)
    chain = None
    interface_maps = []
    for k in range(LEVELS):
        child = split(jnp.where(bits[k] == 0, child_ref[k, :, :128], child_ref[k, :, 128:]))
        sign = (1 - 2 * bits[k]).astype(F32)
        step = mi_ref[k] if chain is None else dot3(split(mi_ref[k]), chain)
        interface_maps.append(step * sign)
        chain = child if chain is None else split(dot3(child, chain))
    interface_map = split(jnp.concatenate(interface_maps, axis=0))
    for part in range(8):
        at = slice(256 * part, 256 * part + 256)
        high, low = split(dot3(split(top_ref[at, :]), chain))
        top_h[at, :] = high
        top_l[at, :] = low
    arrived(11, 9, 10)
    extend = dot3(split(ext_t_ref[...].T), split(spr_e_ref[...]))
    spread_h, spread_low = split(spr_l_ref[...])
    spread_twice = jnp.concatenate([spread_h, spread_h], axis=1)

    for copy in gathers:
        copy.wait_recv()
    x = dst3[...].reshape(4 * N_COL, 128)
    differences = []
    for k in range(LEVELS):
        rows = (4 * N_COL) >> (k + 1)
        first, second = x[:rows], x[rows:]
        differences.append((second - first)[:4])
        joined = jnp.concatenate([first, second], axis=1)
        x = few_rows_dot3(joined, (par_h[k], par_l[k]))
    src4[...] = x
    dst4[row] = x
    sends = []
    arrivals = []
    for d in range(1, N_ROW):
        sends.append(remote(src4, dst4.at[row], send4.at[d], recv4.at[d], (row_at(d), col)))
        arrivals.append(
            remote(src4, dst4.at[row_at(N_ROW - d)], send4.at[d], recv4.at[d], (row_at(d), col))
        )
    for copy in sends:
        copy.start()
    boundary = few_rows_dot3(jnp.concatenate(differences, axis=1), interface_map)
    for copy in gathers + sends:
        copy.wait_send()
    for copy in arrivals:
        copy.wait_recv()
    pieces = jnp.concatenate([dst4[g] for g in range(N_ROW)], axis=1)
    boundary = boundary + few_rows_dot3(pieces, (top_h[...], top_l[...]))
    for f in range(4):
        weighted = split(extend * boundary[f : f + 1, :])
        at = slice(256 * f, 256 * f + 256)
        edges = mm(jnp.concatenate(weighted, axis=1), spread_twice, ((1,), (1,)))
        edges = edges + mm(weighted[0], spread_low, ((1,), (1,)))
        out_ref[at, :] = (part_ref[at, :] + edges).astype(BF16)


def local(
    state_fields, leaf_solve, leaf_flux, lift_edges, lift_leaves, merge_interface, merge_parent,
    split_child, top_inverse, spread_edges, spread_leaves, leaf_extend,
):
    der_h, der_l = derivative_parts()
    dma = pltpu.SemaphoreType.DMA
    args = (
        state_fields.reshape(1024, 256), leaf_solve, leaf_flux, lift_edges, lift_leaves,
        merge_interface, merge_parent, split_child, top_inverse, spread_edges, spread_leaves,
        leaf_extend.T, jnp.asarray(der_h), jnp.asarray(der_l), jnp.asarray(face_columns()),
    )
    result = pl.pallas_call(
        kernel,
        name="imex_step",
        out_shape=jax.ShapeDtypeStruct((1024, 256), BF16),
        in_specs=[pl.BlockSpec(memory_space=pltpu.HBM)] * 15,
        out_specs=pl.BlockSpec(memory_space=pltpu.VMEM),
        scratch_shapes=[pltpu.VMEM(a.shape, a.dtype) for a in args]
        + [
            dma((15,)),
            pltpu.VMEM((1024, 256), F32),
            pltpu.VMEM((1024, 256), F32),
            pltpu.VMEM((256, 128), F32),
            pltpu.VMEM((2, 64, 128), F32),
            pltpu.VMEM((2, 64, 128), F32),
            pltpu.VMEM((2, 64, 128), F32),
            pltpu.VMEM((2, 64, 128), F32),
            pltpu.VMEM((4, 128), F32),
            pltpu.VMEM((N_COL, 4, 128), F32),
            pltpu.VMEM((4, 128), F32),
            pltpu.VMEM((N_ROW, 4, 128), F32),
            pltpu.VMEM((4, 4, 128), F32),
            pltpu.VMEM((4, 4, 128), F32),
            pltpu.VMEM((LEVELS, 256, 128), BF16),
            pltpu.VMEM((LEVELS, 256, 128), BF16),
            pltpu.VMEM((2048, 128), BF16),
            pltpu.VMEM((2048, 128), BF16),
            dma((2,)), dma((2,)), dma((2,)), dma((2,)),
            dma((N_COL,)), dma((N_COL,)), dma((N_ROW,)), dma((N_ROW,)), dma((4,)), dma((4,)),
        ],
        compiler_params=pltpu.CompilerParams(
            collective_id=0, has_side_effects=True, vmem_limit_bytes=48 * 1024 * 1024
        ),
    )(*[pltpu.with_memory_space_constraint(a, pltpu.HBM) for a in args])
    return result.reshape(state_fields.shape)


def solution(mesh):
    in_specs = (
        P(None, None, None, "row", "col", None),
        P(), P(), P(), P(), P(), P(), P(),
        P(None, "row"),
        P(), P(), P(),
    )
    out_specs = P(None, None, None, "row", "col", None)
    return jax.shard_map(local, mesh=mesh, in_specs=in_specs, out_specs=out_specs, check_vma=False)
```

```python
import jax
import jax.numpy as jnp
import numpy as np
from jax import lax
from jax.experimental import pallas as pl
from jax.experimental.pallas import tpu as pltpu
from jax.sharding import PartitionSpec as P

F32 = jnp.float32
BF16 = jnp.bfloat16
MESH = pl.DeviceIdType.MESH
LEVELS = 5
N_ROW = 16
N_COL = 32
advect_scale = 0.01
Y_STEPS = (0, 1, 2, 3, 4, 3, 2, 3)
X_STEPS = (0, 1, 2, 1)
FAR_FIRST = sorted(range(1, N_COL), key=lambda m: -(Y_STEPS[m % 8] + X_STEPS[m // 8]))
ROWS_FAR_FIRST = sorted(range(1, N_ROW), key=lambda d: -min(d, N_ROW - d))


def chebyshev_matrix(node_count):
    points = np.arange(node_count)
    grid_x = np.cos(np.pi * points / (node_count - 1))
    weights = np.where(points == 0, 2.0, np.where(points == node_count - 1, 2.0, 1.0))
    parity = np.where((points[:, None] + points[None, :]) % 2 == 0, 1.0, -1.0)
    identity = np.eye(node_count)
    spacing = grid_x[:, None] - grid_x[None, :] + identity
    off_diagonal = weights[:, None] / weights[None, :] * parity / spacing * (1.0 - identity)
    result_matrix = off_diagonal - identity * off_diagonal.sum(axis=1)[:, None]
    return result_matrix.astype(np.float32)


def derivative_parts():
    d = chebyshev_matrix(16)
    eye = np.eye(16, dtype=np.float32)
    both = np.concatenate([np.kron(d, eye), np.kron(eye, d)], axis=0) * np.float32(advect_scale)
    high = both.astype(jnp.bfloat16)
    low = (both - high.astype(np.float32)).astype(jnp.bfloat16)
    return high, low


def face_columns():
    e = np.zeros((256, 64), np.float32)
    for k in range(16):
        e[k, k] = 1.0
        e[240 + k, 16 + k] = 1.0
        e[16 * k, 32 + k] = 1.0
        e[16 * k + 15, 48 + k] = 1.0
    return e.astype(jnp.bfloat16)


def split(x):
    high = x.astype(BF16)
    return high, (x - high.astype(F32)).astype(BF16)


def mm(a, b, dims=((1,), (0,))):
    return lax.dot_general(a, b, (dims, ((), ())), preferred_element_type=F32)


def dot3(a, b, dims=((1,), (0,))):
    return mm(a[0], b[0], dims) + mm(a[0], b[1], dims) + mm(a[1], b[0], dims)


def few_rows_dot3(a, b):
    high = a.astype(BF16)
    rows = a.shape[0]
    both = mm(jnp.concatenate([a, a - high.astype(F32)], axis=0).astype(BF16), b[0])
    return both[:rows] + both[rows:] + mm(high, b[1])


def bit_reversed(m):
    return sum(((m >> k) & 1) << (LEVELS - 1 - k) for k in range(LEVELS))


def kernel(*refs):
    stored, out_ref, held, loaded = refs[:15], refs[15], refs[16:31], refs[31]
    step(stored, held, loaded, out_ref, *refs[32:])


def step(
    stored, held, loaded, out_ref,
    tend_ref, part_ref, k_ref, src1, dst1, src2, dst2, src3, dst3, src4, dst4, src6, dst6,
    par_h, par_l, top_h, top_l,
    send1, recv1, send2, recv2, send3, recv3, send4, recv4, send6, recv6,
):
    row = lax.axis_index("row")
    col = lax.axis_index("col")
    bits = [(col // (1 << k)) % 2 for k in range(LEVELS)]

    def other(m):
        return sum(
            (1 - bits[k] if (m >> k) & 1 else bits[k]) * (1 << k) for k in range(LEVELS)
        )

    def row_at(d):
        return (row + d) % N_ROW

    (
        q_ref, solve_ref, flux_ref, lift_e_ref, lift_l_ref, mi_ref, parent_ref, child_ref,
        top_ref, spr_e_ref, spr_l_ref, ext_t_ref, der_h_ref, der_l_ref, face_ref,
    ) = held
    loads = [
        pltpu.make_async_copy(stored[i], held[i], loaded.at[i]) for i in range(15)
    ]
    for i in (0, 12, 13, 2, 3, 4, 6, 1, 14, 5, 7, 8, 11, 9, 10):
        loads[i].start()

    barrier = pltpu.get_barrier_semaphore()
    for m in FAR_FIRST:
        pl.semaphore_signal(barrier, inc=1, device_id=(row, other(m)), device_id_type=MESH)
    for d in ROWS_FAR_FIRST:
        pl.semaphore_signal(barrier, inc=1, device_id=(row_at(d), col), device_id_type=MESH)
    down, up = row_at(1), row_at(N_ROW - 1)
    east_col, west_col = (col + 1) % N_COL, (col + N_COL - 1) % N_COL
    diagonal = [(down, east_col), (down, west_col), (up, east_col), (up, west_col)]
    for peer in diagonal:
        pl.semaphore_signal(barrier, inc=1, device_id=peer, device_id_type=MESH)

    def arrived(*which):
        for i in which:
            loads[i].wait()

    arrived(0, 12, 13)
    der_h, der_l = der_h_ref[...], der_l_ref[...]
    q0 = q_ref[0:256, :].astype(F32)
    q1 = q_ref[256:512, :].astype(F32)
    for f in range(4):
        q = q_ref[256 * f : 256 * f + 256, :]
        both = mm(der_h, q) + mm(der_l, q)
        tend_ref[256 * f : 256 * f + 256, :] = q0 * both[:256] + q1 * both[256:]

    lane = lax.broadcasted_iota(jnp.int32, (64, 256), 1)
    half_lane = lax.broadcasted_iota(jnp.int32, (64, 128), 1)
    place = lax.broadcasted_iota(jnp.int32, (64, 256), 0) % 16

    def rows_of(first):
        return jnp.concatenate(
            [tend_ref[256 * f + first : 256 * f + first + 16, :] for f in range(4)], axis=0
        )

    def nodes_of(first):
        return tend_ref[...].reshape(64, 16, 256)[:, first, :]

    top, bottom = rows_of(0), rows_of(240)
    above = pltpu.roll(bottom, 64, 1)
    below = pltpu.roll(top, 192, 1)
    src1[0] = above[:, :128]
    src1[1] = below[:, 128:]

    left, right = nodes_of(0), nodes_of(15)

    def with_corners(top_rows, bottom_rows):
        left_rows = jnp.where(
            place == 0, top_rows, jnp.where(place == 15, pltpu.roll(bottom_rows, 15, 0), left)
        )
        right_rows = jnp.where(
            place == 0, pltpu.roll(top_rows, 49, 0), jnp.where(place == 15, bottom_rows, right)
        )
        return left_rows, right_rows

    left_part, right_part = with_corners(
        (top + jnp.where(lane < 64, 0.0, above)) * 0.5,
        (bottom + jnp.where(lane >= 192, 0.0, below)) * 0.5,
    )
    to_east = pltpu.roll(right_part, 193, 1)
    to_west = pltpu.roll(left_part, 63, 1)
    src2[0] = jnp.where(half_lane % 64 == 0, to_east[:, :128], pltpu.roll(to_east[:, 128:], 1, 1))
    src2[1] = jnp.where(half_lane % 64 == 63, to_west[:, :128], pltpu.roll(to_west[:, 128:], 1, 1))

    def corner(rows, shift, node):
        return pltpu.roll(rows, shift, 1).reshape(4, 16, 128)[:, node, :]

    src6[0] = corner(above[:, :128], 65, 15)
    src6[1] = corner(above[:, :128], 63, 0)
    src6[2] = corner(below[:, 128:], 65, 15)
    src6[3] = corner(below[:, 128:], 63, 0)
    pl.semaphore_wait(barrier, N_COL - 1 + N_ROW - 1 + 4)

    def remote(src, dst, send, recv, where):
        return pltpu.make_async_remote_copy(
            src_ref=src, dst_ref=dst, send_sem=send, recv_sem=recv, device_id=where,
            device_id_type=MESH,
        )

    faces = [
        remote(src6.at[k], dst6.at[k], send6.at[k], recv6.at[k], diagonal[k]) for k in range(4)
    ]
    faces += [
        remote(src2.at[0], dst2.at[0], send2.at[0], recv2.at[0], (row, east_col)),
        remote(src2.at[1], dst2.at[1], send2.at[1], recv2.at[1], (row, west_col)),
        remote(src1.at[0], dst1.at[0], send1.at[0], recv1.at[0], (down, col)),
        remote(src1.at[1], dst1.at[1], send1.at[1], recv1.at[1], (up, col)),
    ]
    for copy in faces:
        copy.start()

    arrived(2, 3, 4)
    k_map = dot3(
        split(flux_ref[...].T), split(lift_e_ref[...])
    )
    k_ref[...] = k_map
    lift_l = split(lift_l_ref[...])
    own = []
    for f in range(4):
        q = q_ref[256 * f : 256 * f + 256, :].astype(F32)
        w = dot3(split(q - tend_ref[256 * f : 256 * f + 256, :]), lift_l)
        own.append(jnp.sum(w * k_map, axis=0, keepdims=True))
    arrived(6)
    for k in range(LEVELS):
        whole = parent_ref[k]
        swapped = jnp.concatenate([whole[128:], whole[:128]], axis=0)
        high, low = split(jnp.where(bits[k] == 0, whole, swapped))
        par_h[k] = high
        par_l[k] = low

    for copy in faces:
        copy.wait()
    above = jnp.where(lane < 64, jnp.concatenate([dst1[0], dst1[0]], axis=1), above)
    below = jnp.where(lane >= 192, jnp.concatenate([dst1[1], dst1[1]], axis=1), below)
    top_new = (top + above) * 0.5
    bottom_new = (bottom + below) * 0.5
    left_rows, right_rows = with_corners(top_new, bottom_new)

    def opened(received):
        return jnp.concatenate([received, pltpu.roll(received, 127, 1)], axis=1)

    def spread_corner(k, node, at):
        rows = dst6[k]
        rows = jnp.concatenate(
            [jnp.broadcast_to(rows[f : f + 1], (16, 128)) for f in range(4)], axis=0
        )
        here = jnp.logical_and(place == node, lane == at)
        return jnp.where(here, jnp.concatenate([rows, rows], axis=1) * 0.5, 0.0)

    before = jnp.where(lane % 64 == 0, opened(dst2[0]), pltpu.roll(right_rows, 1, 1))
    before = before + spread_corner(0, 0, 0) + spread_corner(2, 15, 192)
    after = jnp.where(lane % 64 == 63, opened(dst2[1]), pltpu.roll(left_rows, 255, 1))
    after = after + spread_corner(1, 0, 63) + spread_corner(3, 15, 255)
    inner = jnp.logical_and(place != 0, place != 15)
    deltas = [
        jnp.where(inner, top_new - top, 0.0),
        jnp.where(inner, bottom_new - bottom, 0.0),
        (left_rows + before) * 0.5 - left,
        (right_rows + after) * 0.5 - right,
    ]
    w = dot3(split(jnp.concatenate(deltas, axis=0)), lift_l)
    k_nodes = k_ref[...].reshape(16, 16, 128)
    k_faces = [k_nodes[0], k_nodes[15], k_nodes[:, 0, :], k_nodes[:, 15, :]]
    skeleton = []
    for f in range(4):
        change = sum(
            w[64 * s + 16 * f : 64 * s + 16 * f + 16] * k_faces[s] for s in range(4)
        )
        skeleton.append(own[f] - jnp.sum(change, axis=0, keepdims=True))
    skeleton = jnp.concatenate(skeleton, axis=0)
    src3[...] = skeleton
    dst3[0] = skeleton
    gathers = []
    for m in FAR_FIRST:
        slot = bit_reversed(m)
        gathers.append(
            remote(src3, dst3.at[slot], send3.at[m], recv3.at[m], (row, other(m)))
        )
    for copy in gathers:
        copy.start()

    arrived(1, 14)
    solve = split(solve_ref[...])
    face = face_ref[...]
    solve_face = (mm(solve[0], face).astype(BF16), mm(solve[1], face).astype(BF16))
    for f in range(4):
        q = q_ref[256 * f : 256 * f + 256, :].astype(F32)
        change = jnp.concatenate([d[16 * f : 16 * f + 16] for d in deltas], axis=0)
        part_ref[256 * f : 256 * f + 256, :] = dot3(
            solve, split(q - tend_ref[256 * f : 256 * f + 256, :])
        ) - dot3(solve_face, split(change))
    arrived(5, 7, 8)
    chain = None
    interface_maps = []
    for k in range(LEVELS):
        child = split(jnp.where(bits[k] == 0, child_ref[k, :, :128], child_ref[k, :, 128:]))
        sign = (1 - 2 * bits[k]).astype(F32)
        step = mi_ref[k] if chain is None else dot3(split(mi_ref[k]), chain)
        interface_maps.append(step * sign)
        chain = child if chain is None else split(dot3(child, chain))
    interface_map = split(jnp.concatenate(interface_maps, axis=0))
    for part in range(8):
        at = slice(256 * part, 256 * part + 256)
        high, low = split(dot3(split(top_ref[at, :]), chain))
        top_h[at, :] = high
        top_l[at, :] = low
    arrived(11, 9, 10)
    extend = dot3(split(ext_t_ref[...].T), split(spr_e_ref[...]))
    spread_h, spread_low = split(spr_l_ref[...])
    spread_twice = jnp.concatenate([spread_h, spread_h], axis=1)

    for copy in gathers:
        copy.wait_recv()
    x = dst3[...].reshape(4 * N_COL, 128)
    differences = []
    for k in range(LEVELS):
        rows = (4 * N_COL) >> (k + 1)
        first, second = x[:rows], x[rows:]
        differences.append((second - first)[:4])
        joined = jnp.concatenate([first, second], axis=1)
        x = few_rows_dot3(joined, (par_h[k], par_l[k]))
    src4[...] = x
    dst4[row] = x
    sends = []
    arrivals = {}
    for d in ROWS_FAR_FIRST:
        sends.append(remote(src4, dst4.at[row], send4.at[d], recv4.at[d], (row_at(d), col)))
        arrivals[d] = remote(
            src4, dst4.at[row_at(N_ROW - d)], send4.at[d], recv4.at[d], (row_at(d), col)
        )
    for copy in sends:
        copy.start()
    boundary = few_rows_dot3(jnp.concatenate(differences, axis=1), interface_map)

    def solved_from(steps):
        rows = [row_at(N_ROW - d) for d in steps]
        spans = [pl.ds(pl.multiple_of(g * 128, 128), 128) for g in rows]
        operator = [
            jnp.concatenate([ref[span, :] for span in spans], axis=0) for ref in (top_h, top_l)
        ]
        return few_rows_dot3(jnp.concatenate([dst4[g] for g in rows], axis=1), operator)

    far, near = ROWS_FAR_FIRST[:3], ROWS_FAR_FIRST[3:]
    for copy in gathers + sends:
        copy.wait_send()
    for d in near:
        arrivals[d].wait_recv()
    boundary = boundary + solved_from([N_ROW] + near)
    for d in far:
        arrivals[d].wait_recv()
    boundary = boundary + solved_from(far)
    for f in range(4):
        weighted = split(extend * boundary[f : f + 1, :])
        at = slice(256 * f, 256 * f + 256)
        edges = mm(jnp.concatenate(weighted, axis=1), spread_twice, ((1,), (1,)))
        edges = edges + mm(weighted[0], spread_low, ((1,), (1,)))
        out_ref[at, :] = (part_ref[at, :] + edges).astype(BF16)


def local(
    state_fields, leaf_solve, leaf_flux, lift_edges, lift_leaves, merge_interface, merge_parent,
    split_child, top_inverse, spread_edges, spread_leaves, leaf_extend,
):
    der_h, der_l = derivative_parts()
    dma = pltpu.SemaphoreType.DMA
    args = (
        state_fields.reshape(1024, 256), leaf_solve, leaf_flux, lift_edges, lift_leaves,
        merge_interface, merge_parent, split_child, top_inverse, spread_edges, spread_leaves,
        leaf_extend.T, jnp.asarray(der_h), jnp.asarray(der_l), jnp.asarray(face_columns()),
    )
    result = pl.pallas_call(
        kernel,
        name="imex_step",
        out_shape=jax.ShapeDtypeStruct((1024, 256), BF16),
        in_specs=[pl.BlockSpec(memory_space=pltpu.HBM)] * 15,
        out_specs=pl.BlockSpec(memory_space=pltpu.VMEM),
        scratch_shapes=[pltpu.VMEM(a.shape, a.dtype) for a in args]
        + [
            dma((15,)),
            pltpu.VMEM((1024, 256), F32),
            pltpu.VMEM((1024, 256), F32),
            pltpu.VMEM((256, 128), F32),
            pltpu.VMEM((2, 64, 128), F32),
            pltpu.VMEM((2, 64, 128), F32),
            pltpu.VMEM((2, 64, 128), F32),
            pltpu.VMEM((2, 64, 128), F32),
            pltpu.VMEM((4, 128), F32),
            pltpu.VMEM((N_COL, 4, 128), F32),
            pltpu.VMEM((4, 128), F32),
            pltpu.VMEM((N_ROW, 4, 128), F32),
            pltpu.VMEM((4, 4, 128), F32),
            pltpu.VMEM((4, 4, 128), F32),
            pltpu.VMEM((LEVELS, 256, 128), BF16),
            pltpu.VMEM((LEVELS, 256, 128), BF16),
            pltpu.VMEM((2048, 128), BF16),
            pltpu.VMEM((2048, 128), BF16),
            dma((2,)), dma((2,)), dma((2,)), dma((2,)),
            dma((N_COL,)), dma((N_COL,)), dma((N_ROW,)), dma((N_ROW,)), dma((4,)), dma((4,)),
        ],
        compiler_params=pltpu.CompilerParams(
            collective_id=0, has_side_effects=True, vmem_limit_bytes=48 * 1024 * 1024
        ),
    )(*[pltpu.with_memory_space_constraint(a, pltpu.HBM) for a in args])
    return result.reshape(state_fields.shape)


def solution(mesh):
    in_specs = (
        P(None, None, None, "row", "col", None),
        P(), P(), P(), P(), P(), P(), P(),
        P(None, "row"),
        P(), P(), P(),
    )
    out_specs = P(None, None, None, "row", "col", None)
    return jax.shard_map(local, mesh=mesh, in_specs=in_specs, out_specs=out_specs, check_vma=False)
```

```python
import jax
import jax.numpy as jnp
import numpy as np
from jax import lax
from jax.experimental import pallas as pl
from jax.experimental.pallas import tpu as pltpu
from jax.sharding import PartitionSpec as P

F32 = jnp.float32
BF16 = jnp.bfloat16
MESH = pl.DeviceIdType.MESH
LEVELS = 5
N_ROW = 16
N_COL = 32
advect_scale = 0.01
Y_STEPS = (0, 1, 2, 3, 4, 3, 2, 3)
X_STEPS = (0, 1, 2, 1)
FAR_FIRST = sorted(range(1, N_COL), key=lambda m: -(Y_STEPS[m % 8] + X_STEPS[m // 8]))
ROWS_FAR_FIRST = sorted(range(1, N_ROW), key=lambda d: -min(d, N_ROW - d))


def chebyshev_matrix(node_count):
    points = np.arange(node_count)
    grid_x = np.cos(np.pi * points / (node_count - 1))
    weights = np.where(points == 0, 2.0, np.where(points == node_count - 1, 2.0, 1.0))
    parity = np.where((points[:, None] + points[None, :]) % 2 == 0, 1.0, -1.0)
    identity = np.eye(node_count)
    spacing = grid_x[:, None] - grid_x[None, :] + identity
    off_diagonal = weights[:, None] / weights[None, :] * parity / spacing * (1.0 - identity)
    result_matrix = off_diagonal - identity * off_diagonal.sum(axis=1)[:, None]
    return result_matrix.astype(np.float32)


def derivative_parts():
    d = chebyshev_matrix(16)
    eye = np.eye(16, dtype=np.float32)
    both = np.concatenate([np.kron(d, eye), np.kron(eye, d)], axis=0) * np.float32(advect_scale)
    high = both.astype(jnp.bfloat16)
    low = (both - high.astype(np.float32)).astype(jnp.bfloat16)
    return high, low


def face_columns():
    e = np.zeros((256, 64), np.float32)
    for k in range(16):
        e[k, k] = 1.0
        e[240 + k, 16 + k] = 1.0
        e[16 * k, 32 + k] = 1.0
        e[16 * k + 15, 48 + k] = 1.0
    return e.astype(jnp.bfloat16)


def split(x):
    high = x.astype(BF16)
    return high, (x - high.astype(F32)).astype(BF16)


def mm(a, b, dims=((1,), (0,))):
    return lax.dot_general(a, b, (dims, ((), ())), preferred_element_type=F32)


def dot3(a, b, dims=((1,), (0,))):
    return mm(a[0], b[0], dims) + mm(a[0], b[1], dims) + mm(a[1], b[0], dims)


def few_rows_dot3(a, b):
    high = a.astype(BF16)
    rows = a.shape[0]
    both = mm(jnp.concatenate([a, a - high.astype(F32)], axis=0).astype(BF16), b[0])
    return both[:rows] + both[rows:] + mm(high, b[1])


def bit_reversed(m):
    return sum(((m >> k) & 1) << (LEVELS - 1 - k) for k in range(LEVELS))


def kernel(*refs):
    stored, out_ref, held, loaded = refs[:15], refs[15], refs[16:31], refs[31]
    step(stored, held, loaded, out_ref, *refs[32:])


def step(
    stored, held, loaded, out_ref,
    tend_ref, part_ref, k_ref, src1, dst1, src2, dst2, src3, dst3, src4, dst4, src6, dst6,
    par_h, par_l, top_h, top_l,
    send1, recv1, send2, recv2, send3, recv3, send4, recv4, send6, recv6,
):
    row = lax.axis_index("row")
    col = lax.axis_index("col")
    bits = [(col // (1 << k)) % 2 for k in range(LEVELS)]

    def other(m):
        return sum(
            (1 - bits[k] if (m >> k) & 1 else bits[k]) * (1 << k) for k in range(LEVELS)
        )

    def row_at(d):
        return (row + d) % N_ROW

    (
        q_ref, solve_ref, flux_ref, lift_e_ref, lift_l_ref, mi_ref, parent_ref, child_ref,
        top_ref, spr_e_ref, spr_l_ref, ext_t_ref, der_h_ref, der_l_ref, face_ref,
    ) = held
    loads = [
        pltpu.make_async_copy(stored[i], held[i], loaded.at[i]) for i in range(15)
    ]
    for i in (0, 12, 13, 2, 3, 4, 6, 1, 14, 5, 7, 8, 11, 9, 10):
        loads[i].start()

    barrier = pltpu.get_barrier_semaphore()
    for m in FAR_FIRST:
        pl.semaphore_signal(barrier, inc=1, device_id=(row, other(m)), device_id_type=MESH)
    for d in ROWS_FAR_FIRST:
        pl.semaphore_signal(barrier, inc=1, device_id=(row_at(d), col), device_id_type=MESH)
    down, up = row_at(1), row_at(N_ROW - 1)
    east_col, west_col = (col + 1) % N_COL, (col + N_COL - 1) % N_COL
    diagonal = [(down, east_col), (down, west_col), (up, east_col), (up, west_col)]
    for peer in diagonal:
        pl.semaphore_signal(barrier, inc=1, device_id=peer, device_id_type=MESH)

    def arrived(*which):
        for i in which:
            loads[i].wait()

    arrived(0, 12, 13)
    der_h, der_l = der_h_ref[...], der_l_ref[...]
    q0 = q_ref[0:256, :].astype(F32)
    q1 = q_ref[256:512, :].astype(F32)
    for f in range(4):
        q = q_ref[256 * f : 256 * f + 256, :]
        both = mm(der_h, q) + mm(der_l, q)
        tend_ref[256 * f : 256 * f + 256, :] = q0 * both[:256] + q1 * both[256:]

    lane = lax.broadcasted_iota(jnp.int32, (64, 256), 1)
    half_lane = lax.broadcasted_iota(jnp.int32, (64, 128), 1)
    place = lax.broadcasted_iota(jnp.int32, (64, 256), 0) % 16

    def rows_of(first):
        return jnp.concatenate(
            [tend_ref[256 * f + first : 256 * f + first + 16, :] for f in range(4)], axis=0
        )

    def nodes_of(first):
        return tend_ref[...].reshape(64, 16, 256)[:, first, :]

    top, bottom = rows_of(0), rows_of(240)
    above = pltpu.roll(bottom, 64, 1)
    below = pltpu.roll(top, 192, 1)
    src1[0] = above[:, :128].astype(BF16)
    src1[1] = below[:, 128:].astype(BF16)

    left, right = nodes_of(0), nodes_of(15)

    def with_corners(top_rows, bottom_rows):
        left_rows = jnp.where(
            place == 0, top_rows, jnp.where(place == 15, pltpu.roll(bottom_rows, 15, 0), left)
        )
        right_rows = jnp.where(
            place == 0, pltpu.roll(top_rows, 49, 0), jnp.where(place == 15, bottom_rows, right)
        )
        return left_rows, right_rows

    left_part, right_part = with_corners(
        (top + jnp.where(lane < 64, 0.0, above)) * 0.5,
        (bottom + jnp.where(lane >= 192, 0.0, below)) * 0.5,
    )
    to_east = pltpu.roll(right_part, 193, 1)
    to_west = pltpu.roll(left_part, 63, 1)
    src2[0] = jnp.where(
        half_lane % 64 == 0, to_east[:, :128], pltpu.roll(to_east[:, 128:], 1, 1)
    ).astype(BF16)
    src2[1] = jnp.where(
        half_lane % 64 == 63, to_west[:, :128], pltpu.roll(to_west[:, 128:], 1, 1)
    ).astype(BF16)

    def corner(rows, shift, node):
        return pltpu.roll(rows, shift, 1).reshape(4, 16, 128)[:, node, :]

    src6[0] = corner(above[:, :128], 65, 15)
    src6[1] = corner(above[:, :128], 63, 0)
    src6[2] = corner(below[:, 128:], 65, 15)
    src6[3] = corner(below[:, 128:], 63, 0)
    pl.semaphore_wait(barrier, N_COL - 1 + N_ROW - 1 + 4)

    def remote(src, dst, send, recv, where):
        return pltpu.make_async_remote_copy(
            src_ref=src, dst_ref=dst, send_sem=send, recv_sem=recv, device_id=where,
            device_id_type=MESH,
        )

    faces = [
        remote(src6.at[k], dst6.at[k], send6.at[k], recv6.at[k], diagonal[k]) for k in range(4)
    ]
    faces += [
        remote(src2.at[0], dst2.at[0], send2.at[0], recv2.at[0], (row, east_col)),
        remote(src2.at[1], dst2.at[1], send2.at[1], recv2.at[1], (row, west_col)),
        remote(src1.at[0], dst1.at[0], send1.at[0], recv1.at[0], (down, col)),
        remote(src1.at[1], dst1.at[1], send1.at[1], recv1.at[1], (up, col)),
    ]
    for copy in faces:
        copy.start()

    arrived(2, 3, 4)
    k_map = dot3(
        split(flux_ref[...].T), split(lift_e_ref[...])
    )
    k_ref[...] = k_map
    lift_l = split(lift_l_ref[...])
    own = []
    for f in range(4):
        q = q_ref[256 * f : 256 * f + 256, :].astype(F32)
        w = dot3(split(q - tend_ref[256 * f : 256 * f + 256, :]), lift_l)
        own.append(jnp.sum(w * k_map, axis=0, keepdims=True))
    arrived(6)
    for k in range(LEVELS):
        whole = parent_ref[k]
        swapped = jnp.concatenate([whole[128:], whole[:128]], axis=0)
        high, low = split(jnp.where(bits[k] == 0, whole, swapped))
        par_h[k] = high
        par_l[k] = low

    for copy in faces:
        copy.wait()
    above = jnp.where(lane < 64, jnp.concatenate([dst1[0], dst1[0]], axis=1).astype(F32), above)
    below = jnp.where(lane >= 192, jnp.concatenate([dst1[1], dst1[1]], axis=1).astype(F32), below)
    top_new = (top + above) * 0.5
    bottom_new = (bottom + below) * 0.5
    left_rows, right_rows = with_corners(top_new, bottom_new)

    def opened(received):
        return jnp.concatenate([received, pltpu.roll(received, 127, 1)], axis=1)

    def spread_corner(k, node, at):
        rows = dst6[k]
        rows = jnp.concatenate(
            [jnp.broadcast_to(rows[f : f + 1], (16, 128)) for f in range(4)], axis=0
        )
        here = jnp.logical_and(place == node, lane == at)
        return jnp.where(here, jnp.concatenate([rows, rows], axis=1) * 0.5, 0.0)

    before = jnp.where(lane % 64 == 0, opened(dst2[0].astype(F32)), pltpu.roll(right_rows, 1, 1))
    before = before + spread_corner(0, 0, 0) + spread_corner(2, 15, 192)
    after = jnp.where(lane % 64 == 63, opened(dst2[1].astype(F32)), pltpu.roll(left_rows, 255, 1))
    after = after + spread_corner(1, 0, 63) + spread_corner(3, 15, 255)
    inner = jnp.logical_and(place != 0, place != 15)
    deltas = [
        jnp.where(inner, top_new - top, 0.0),
        jnp.where(inner, bottom_new - bottom, 0.0),
        (left_rows + before) * 0.5 - left,
        (right_rows + after) * 0.5 - right,
    ]
    w = dot3(split(jnp.concatenate(deltas, axis=0)), lift_l)
    k_nodes = k_ref[...].reshape(16, 16, 128)
    k_faces = [k_nodes[0], k_nodes[15], k_nodes[:, 0, :], k_nodes[:, 15, :]]
    skeleton = []
    for f in range(4):
        change = sum(
            w[64 * s + 16 * f : 64 * s + 16 * f + 16] * k_faces[s] for s in range(4)
        )
        skeleton.append(own[f] - jnp.sum(change, axis=0, keepdims=True))
    skeleton = jnp.concatenate(skeleton, axis=0)
    src3[...] = skeleton
    dst3[0] = skeleton
    gathers = []
    for m in FAR_FIRST:
        slot = bit_reversed(m)
        gathers.append(
            remote(src3, dst3.at[slot], send3.at[m], recv3.at[m], (row, other(m)))
        )
    for copy in gathers:
        copy.start()

    arrived(1, 14)
    solve = split(solve_ref[...])
    face = face_ref[...]
    solve_face = (mm(solve[0], face).astype(BF16), mm(solve[1], face).astype(BF16))
    for f in range(4):
        q = q_ref[256 * f : 256 * f + 256, :].astype(F32)
        change = jnp.concatenate([d[16 * f : 16 * f + 16] for d in deltas], axis=0)
        part_ref[256 * f : 256 * f + 256, :] = dot3(
            solve, split(q - tend_ref[256 * f : 256 * f + 256, :])
        ) - dot3(solve_face, split(change))
    arrived(5, 7, 8)
    chain = None
    interface_maps = []
    for k in range(LEVELS):
        child = split(jnp.where(bits[k] == 0, child_ref[k, :, :128], child_ref[k, :, 128:]))
        sign = (1 - 2 * bits[k]).astype(F32)
        step = mi_ref[k] if chain is None else dot3(split(mi_ref[k]), chain)
        interface_maps.append(step * sign)
        chain = child if chain is None else split(dot3(child, chain))
    interface_map = split(jnp.concatenate(interface_maps, axis=0))
    for part in range(8):
        at = slice(256 * part, 256 * part + 256)
        high, low = split(dot3(split(top_ref[at, :]), chain))
        top_h[at, :] = high
        top_l[at, :] = low
    arrived(11, 9, 10)
    extend = dot3(split(ext_t_ref[...].T), split(spr_e_ref[...]))
    spread_h, spread_low = split(spr_l_ref[...])
    spread_twice = jnp.concatenate([spread_h, spread_h], axis=1)

    for copy in gathers:
        copy.wait_recv()
    x = dst3[...].reshape(4 * N_COL, 128)
    differences = []
    for k in range(LEVELS):
        rows = (4 * N_COL) >> (k + 1)
        first, second = x[:rows], x[rows:]
        differences.append((second - first)[:4])
        joined = jnp.concatenate([first, second], axis=1)
        x = few_rows_dot3(joined, (par_h[k], par_l[k]))
    src4[...] = x
    dst4[row] = x
    sends = []
    arrivals = {}
    for d in ROWS_FAR_FIRST:
        sends.append(remote(src4, dst4.at[row], send4.at[d], recv4.at[d], (row_at(d), col)))
        arrivals[d] = remote(
            src4, dst4.at[row_at(N_ROW - d)], send4.at[d], recv4.at[d], (row_at(d), col)
        )
    for copy in sends:
        copy.start()
    boundary = few_rows_dot3(jnp.concatenate(differences, axis=1), interface_map)

    def solved_from(steps):
        rows = [row_at(N_ROW - d) for d in steps]
        spans = [pl.ds(pl.multiple_of(g * 128, 128), 128) for g in rows]
        operator = [
            jnp.concatenate([ref[span, :] for span in spans], axis=0) for ref in (top_h, top_l)
        ]
        return few_rows_dot3(jnp.concatenate([dst4[g] for g in rows], axis=1), operator)

    far, near = ROWS_FAR_FIRST[:3], ROWS_FAR_FIRST[3:]
    for copy in gathers + sends:
        copy.wait_send()
    for d in near:
        arrivals[d].wait_recv()
    boundary = boundary + solved_from([N_ROW] + near)
    for d in far:
        arrivals[d].wait_recv()
    boundary = boundary + solved_from(far)
    for f in range(4):
        weighted = split(extend * boundary[f : f + 1, :])
        at = slice(256 * f, 256 * f + 256)
        edges = mm(jnp.concatenate(weighted, axis=1), spread_twice, ((1,), (1,)))
        edges = edges + mm(weighted[0], spread_low, ((1,), (1,)))
        out_ref[at, :] = (part_ref[at, :] + edges).astype(BF16)


def local(
    state_fields, leaf_solve, leaf_flux, lift_edges, lift_leaves, merge_interface, merge_parent,
    split_child, top_inverse, spread_edges, spread_leaves, leaf_extend,
):
    der_h, der_l = derivative_parts()
    dma = pltpu.SemaphoreType.DMA
    args = (
        state_fields.reshape(1024, 256), leaf_solve, leaf_flux, lift_edges, lift_leaves,
        merge_interface, merge_parent, split_child, top_inverse, spread_edges, spread_leaves,
        leaf_extend.T, jnp.asarray(der_h), jnp.asarray(der_l), jnp.asarray(face_columns()),
    )
    result = pl.pallas_call(
        kernel,
        name="imex_step",
        out_shape=jax.ShapeDtypeStruct((1024, 256), BF16),
        in_specs=[pl.BlockSpec(memory_space=pltpu.HBM)] * 15,
        out_specs=pl.BlockSpec(memory_space=pltpu.VMEM),
        scratch_shapes=[pltpu.VMEM(a.shape, a.dtype) for a in args]
        + [
            dma((15,)),
            pltpu.VMEM((1024, 256), F32),
            pltpu.VMEM((1024, 256), F32),
            pltpu.VMEM((256, 128), F32),
            pltpu.VMEM((2, 64, 128), BF16),
            pltpu.VMEM((2, 64, 128), BF16),
            pltpu.VMEM((2, 64, 128), BF16),
            pltpu.VMEM((2, 64, 128), BF16),
            pltpu.VMEM((4, 128), F32),
            pltpu.VMEM((N_COL, 4, 128), F32),
            pltpu.VMEM((4, 128), F32),
            pltpu.VMEM((N_ROW, 4, 128), F32),
            pltpu.VMEM((4, 4, 128), F32),
            pltpu.VMEM((4, 4, 128), F32),
            pltpu.VMEM((LEVELS, 256, 128), BF16),
            pltpu.VMEM((LEVELS, 256, 128), BF16),
            pltpu.VMEM((2048, 128), BF16),
            pltpu.VMEM((2048, 128), BF16),
            dma((2,)), dma((2,)), dma((2,)), dma((2,)),
            dma((N_COL,)), dma((N_COL,)), dma((N_ROW,)), dma((N_ROW,)), dma((4,)), dma((4,)),
        ],
        compiler_params=pltpu.CompilerParams(
            collective_id=0, has_side_effects=True, vmem_limit_bytes=48 * 1024 * 1024
        ),
    )(*[pltpu.with_memory_space_constraint(a, pltpu.HBM) for a in args])
    return result.reshape(state_fields.shape)


def solution(mesh):
    in_specs = (
        P(None, None, None, "row", "col", None),
        P(), P(), P(), P(), P(), P(), P(),
        P(None, "row"),
        P(), P(), P(),
    )
    out_specs = P(None, None, None, "row", "col", None)
    return jax.shard_map(local, mesh=mesh, in_specs=in_specs, out_specs=out_specs, check_vma=False)
```
